32 devices in a mesh: fsdp: 2 (over y), ctx: 4 (over x, core), tp: 4 (over z).
Axes of the slice: x: 2, y: 2, z: 4, core: 2. Of those that a mesh axis runs over, the one named last changes fastest.
Arguments:
- tokens: bfloat16 [12608, 512], P(('fsdp', 'ctx', 'tp')), may hold values from -6 to 6
- w_qkv: float32 [512, 1536], P(('fsdp', 'ctx', 'tp')), may hold values from -0.375 to 0.375
- w_attend: float32 [512, 512], P(('fsdp', 'ctx', 'tp')), may hold values from -0.75 to 0.75
- w_route: float32 [512, 8], P(('fsdp', 'ctx', 'tp')), may hold values from -0.1875 to 0.1875
- gain_one: float32 [512], P(('fsdp', 'ctx', 'tp')), may hold values from 0.5 to 1.5
- shift_one: float32 [512], P(('fsdp', 'ctx', 'tp')), may hold values from -1 to 1
- gain_two: float32 [512], P(('fsdp', 'ctx', 'tp')), may hold values from 0.5 to 1.5
- shift_two: float32 [512], P(('fsdp', 'ctx', 'tp')), may hold values from -1 to 1
- w_up: float32 [8, 512, 2048], P(None, ('fsdp', 'ctx'), 'tp'), may hold values from -0.25 to 0.25
- w_down: float32 [8, 512, 2048], P(None, ('fsdp', 'ctx'), 'tp'), may hold values from -0.75 to 0.75
- routes: int32 [12608, 2], P(('fsdp', 'ctx')), may hold values from 0 to 7, all different within a row
- priority: int32 [8, 1576], P(('fsdp', 'ctx')), may hold values from 0 to 1575, each once within a row
- cotangent: bfloat16 [12608, 512], P(('fsdp', 'ctx', 'tp')), may hold values from -6 to 6
Outputs:
- output: bfloat16 [12608, 512], P(('fsdp', 'ctx', 'tp'))
- grad_tokens: bfloat16 [12608, 512], P(('fsdp', 'ctx', 'tp'))
- grad_qkv: float32 [512, 1536], P(('fsdp', 'ctx', 'tp'))
- grad_attend: float32 [512, 512], P(('fsdp', 'ctx', 'tp'))
- grad_route: float32 [512, 8], P(('fsdp', 'ctx', 'tp'))
- grad_gain_one: float32 [512], P(('fsdp', 'ctx', 'tp'))
- grad_shift_one: float32 [512], P(('fsdp', 'ctx', 'tp'))
- grad_gain_two: float32 [512], P(('fsdp', 'ctx', 'tp'))
- grad_shift_two: float32 [512], P(('fsdp', 'ctx', 'tp'))
- grad_up: float32 [8, 512, 2048], P(None, ('fsdp', 'ctx'), 'tp')
- grad_down: float32 [8, 512, 2048], P(None, ('fsdp', 'ctx'), 'tp')
The draws below stay inside these ranges and needn't reach their ends.
Inputs may be any that keep to these rules, and one draw needn't show every extreme that they name: `routes`: each row names 2 different experts, and every expert is named by some row. `priority`: each row is a permutation of 0 to 1575.
All inputs are finite; a program needn't handle non-finite values.
Results may differ from the reference program's by a relative error of at most 0.015.
The reference program's roundings to bfloat16 on the way count: a program that leaves them out, or rounds other values in their place, can miss the bound.
Values may be sent and summed in bfloat16 or wider, within the bound.
No kernel may reach another device: no remote copies, remote signals or barrier semaphores. Data moves between devices by JAX's collectives and lax.ppermute only.
A program may use at most 192 MiB of HBM per device.

```python
import math
import jax
import jax.numpy as jnp
from jax import lax

D = 512
HEADS = 8
HEAD = 64
FF = 2048
SEQ = 197
TOP = 2
EXPERTS = 8
IMAGES = 64
TOKENS = 12608
GROUPS = 8
GROUP = 1576
CAP = 492


def block_levels(key, shape, shards, smallest, top_value):
    level, own = 1.0, jax.random.fold_in(key, 6)
    for dim, blocks in shards:
        draws = jnp.exp(jax.random.uniform(jax.random.fold_in(own, dim), (blocks,), jnp.float32, smallest / len(shards), top_value / len(shards)))
        level = level * jnp.repeat(draws, shape[dim] // blocks).reshape([-1 if axis == dim else 1 for axis in range(len(shape))])
    return level


def distinct(rng, rows, amount, top, lift):
    ranking = jax.random.permutation(jax.random.fold_in(rng, 1), amount)
    boost = ranking
    for power in range(3):
        boost = boost * boost // amount
    boost = boost * lift // amount
    lots = jax.random.randint(jax.random.fold_in(rng, 2), (rows, amount), 0, 4096) + boost
    fixed_rows = jax.random.permutation(jax.random.fold_in(rng, 3), rows)[jnp.arange(amount) % rows]
    lots = jnp.where(jnp.arange(rows)[:, None] == fixed_rows[None, :], 1 << 14, lots)
    score = lots * amount + jnp.arange(amount)
    return lax.top_k(score.astype(jnp.int32), top)[1].astype(jnp.int32)


def gaussian(stream_key, extent, scale, reach, cuts=(), kind=jnp.bfloat16):
    values = jax.random.normal(stream_key, extent, jnp.float32) * scale
    if len(cuts) > 0:
        values = block_levels(stream_key, extent, cuts, -0.22, 0.18) * values
    return jnp.clip(values, min=-reach, max=reach).astype(kind)


def setup_inputs(seed: int = 0) -> dict:
    seeds = jax.random.split(jax.random.key(seed), 14)
    tokens = gaussian(seeds[0], (TOKENS, D), 1.0, 6.0, ((0, 32),))
    w_qkv = gaussian(seeds[1], (D, 3 * D), (D // 2) ** -0.5, 0.375, ((0, 32),), jnp.float32)
    w_attend = gaussian(seeds[2], (D, D), (D // 8) ** -0.5, 0.75, ((0, 32),), jnp.float32)
    w_route = gaussian(seeds[3], (D, EXPERTS), (2 * D) ** -0.5, 0.1875, ((0, 32),), jnp.float32)
    gain_one = jnp.clip(1.0 + 0.1 * jax.random.normal(seeds[4], (D,), jnp.float32), 0.5, 1.5)
    shift_one = gaussian(seeds[5], (D,), 0.2, 1.0, ((0, 32),), jnp.float32)
    gain_two = jnp.clip(1.0 + 0.1 * jax.random.normal(seeds[6], (D,), jnp.float32), 0.5, 1.5)
    shift_two = gaussian(seeds[7], (D,), 0.2, 1.0, ((0, 32),), jnp.float32)
    w_up = gaussian(seeds[8], (EXPERTS, D, FF), D ** -0.5, 0.25, ((1, 8), (2, 4)), jnp.float32)
    w_down = gaussian(seeds[9], (EXPERTS, D, FF), (FF // 32) ** -0.5, 0.75, ((1, 8), (2, 4)), jnp.float32)
    routes = distinct(seeds[10], TOKENS, EXPERTS, TOP, 2048)
    priority = jax.vmap(lambda own: jax.random.permutation(own, GROUP))(jax.random.split(seeds[11], GROUPS)).reshape((GROUPS, GROUP)).astype(jnp.int32)
    cotangent = gaussian(seeds[12], (TOKENS, D), 1.0, 6.0, ((0, 32),))
    return {"tokens": tokens, "w_qkv": w_qkv, "w_attend": w_attend, "w_route": w_route, "gain_one": gain_one, "shift_one": shift_one, "gain_two": gain_two, "shift_two": shift_two, "w_up": w_up, "w_down": w_down, "routes": routes, "priority": priority, "cotangent": cotangent}


@jax.custom_vjp
def low(v):
    return lax.optimization_barrier(v.astype(jnp.bfloat16)).astype(jnp.float32)

@jax.custom_vjp
def low_back(v):
    return v

def low_keep(v):
    return (low(v), None)

def low_pass(kept, grad):
    return (grad,)

def back_keep(v):
    return (v, None)

def back_low(kept, grad):
    return (low(grad),)
low.defvjp(low_keep, low_pass)
low_back.defvjp(back_keep, back_low)
epsilon = 1e-06
highest = lax.Precision.HIGHEST

def layer_norm(values, gain_row, offset):
    center = values - lax.optimization_barrier(jnp.mean(values, axis=-1, keepdims=True))
    spread = lax.optimization_barrier(jnp.mean(center * center, axis=-1, keepdims=True))
    return center * lax.rsqrt(spread + epsilon) * gain_row + offset

def slot_tables(routes_group, order_group, capacity):
    row_count = order_group.shape[0]
    inverse = jnp.zeros((row_count,), jnp.int32).at[order_group].set(jnp.arange(row_count, dtype=jnp.int32))
    ordered = routes_group[inverse].T.reshape(-1)
    expert_ids = jnp.arange(EXPERTS, dtype=jnp.int32)
    onehot = (ordered[:, None] == expert_ids[None, :]).astype(jnp.int32)
    earlier = jnp.cumsum(onehot, axis=0) - onehot
    slot_keyed = lax.optimization_barrier(jnp.sum(earlier * onehot, axis=1)).reshape(TOP, row_count)
    slot_index = slot_keyed[:, order_group].T
    kept_pair = slot_index < capacity
    position = jnp.where(kept_pair, routes_group * capacity + slot_index, 0).astype(jnp.int32)
    target = jnp.where(kept_pair, position, EXPERTS * capacity).reshape(-1)
    owners = jnp.broadcast_to(jnp.arange(row_count, dtype=jnp.int32)[:, None], (row_count, TOP)).reshape(-1)
    slot_table = jnp.full((EXPERTS * capacity,), row_count, jnp.int32).at[target].set(owners, mode='drop')
    return (kept_pair, position, slot_table)

def attend(qkv_block):
    image_count = qkv_block.shape[0] // SEQ
    split_heads = qkv_block.reshape(image_count, SEQ, 3, HEADS, HEAD)
    queries = split_heads[:, :, 0]
    keys_all = split_heads[:, :, 1]
    values_all = split_heads[:, :, 2]
    scores = low_back(jnp.einsum('bqhd,bkhd->bhqk', queries, keys_all, precision=highest) / math.sqrt(HEAD))
    weights_low = low(jax.nn.softmax(scores, axis=-1))
    context = jnp.einsum('bhqk,bkhd->bqhd', weights_low, values_all, precision=highest)
    return context.reshape(image_count * SEQ, D)

def block_forward(floats, routes, priority):
    tokens_f, qkv_w, attend_w, route_w, gain_a, offset_a, gain_b, offset_b, up_w, down_w = floats
    a_one = low(layer_norm(tokens_f, low(gain_a), low(offset_a)))
    projected = low(low_back(jnp.dot(a_one, low(qkv_w), precision=highest)))
    limit = max(1, 4096 // SEQ)
    per_block = max((divisor for divisor in range(1, limit + 1) if IMAGES % divisor == 0))
    blocks = projected.reshape(IMAGES // per_block, per_block * SEQ, 3 * D)
    context = lax.map(jax.checkpoint(attend), blocks).reshape(TOKENS, D)
    context = low(low_back(context))
    branch = low_back(jnp.dot(context, low(attend_w), precision=highest))
    y_one = tokens_f + branch
    a_two = low(layer_norm(y_one, low(gain_b), low(offset_b)))
    logits = low_back(jnp.dot(a_two, low(route_w), precision=highest))
    gate_probs = jax.nn.softmax(logits, axis=-1)
    up_low = low(up_w)
    down_low = low(down_w)

    def expert_group(pieces):
        a_group, gate_group, route_group, order_group = pieces
        kept_pair, position, slot_table = slot_tables(route_group, order_group, CAP)
        padded = jnp.concatenate([a_group, jnp.zeros((1, D), jnp.float32)], axis=0)
        expert_in = padded[slot_table].reshape(EXPERTS, CAP, D)
        pre_act = low_back(jnp.einsum('ecd,edf->ecf', expert_in, up_low, precision=highest))
        hidden = low(jax.nn.gelu(pre_act, approximate=True))
        expert_out = low_back(jnp.einsum('ecf,edf->ecd', hidden, down_low, precision=highest))
        picked = expert_out.reshape(EXPERTS * CAP, D)[position]
        route_onehot = (route_group[:, :, None] == jnp.arange(EXPERTS, dtype=jnp.int32)[None, None, :]).astype(jnp.float32)
        chosen = lax.optimization_barrier(jnp.sum(gate_group[:, None, :] * route_onehot, axis=-1))
        weight_pair = jnp.where(kept_pair, chosen, 0.0)
        return lax.optimization_barrier(jnp.sum(picked * weight_pair[:, :, None], axis=1))
    moe_rows = lax.map(jax.checkpoint(expert_group), (a_two.reshape(GROUPS, GROUP, D), gate_probs.reshape(GROUPS, GROUP, EXPERTS), routes.reshape(GROUPS, GROUP, TOP), priority))
    return y_one + moe_rows.reshape(TOKENS, D)

def reference(tokens, w_qkv, w_attend, w_route, gain_one, shift_one, gain_two, shift_two, w_up, w_down, routes, priority, cotangent):
    floats = tuple((array.astype(jnp.float32) for array in (tokens, w_qkv, w_attend, w_route, gain_one, shift_one, gain_two, shift_two, w_up, w_down)))
    result, pullback = jax.vjp(lambda *values: block_forward(values, routes, priority), *floats)
    gradients = pullback(cotangent.astype(jnp.float32))
    return (result.astype(jnp.bfloat16), gradients[0].astype(jnp.bfloat16), gradients[1], gradients[2], gradients[3], gradients[4], gradients[5], gradients[6], gradients[7], gradients[8], gradients[9])
```

```python
from functools import partial
import math

import jax
import jax.numpy as jnp
from jax import lax
from jax.experimental import pallas as pl
from jax.experimental.pallas import tpu as pltpu
from jax.sharding import PartitionSpec as P

D = 512
HEADS = 8
HEAD = 64
SEQ = 197
TOP = 2
EXPERTS = 8

LANES = 128
ROWS = 208
WIDE = 3 * D + D + LANES
SIDE = 4 * D

epsilon = 1e-06
low_type = jnp.bfloat16
full_type = jnp.float32
ALL_AXES = ("fsdp", "ctx", "tp")
ROW_AXES = ("fsdp", "ctx")
VMEM_LIMIT = 58 * 1024 * 1024


def norm_forward(values):
    center = values - jnp.mean(values, axis=-1, keepdims=True)
    spread = jnp.mean(center * center, axis=-1, keepdims=True)
    inv_scale = lax.rsqrt(spread + epsilon)
    return (center * inv_scale, inv_scale)


def norm_backward(grad_norm, normed, inv_scale, gain_row):
    scaled = grad_norm * gain_row
    centred = scaled - jnp.mean(scaled, axis=-1, keepdims=True)
    return inv_scale * (centred - normed * jnp.mean(scaled * normed, axis=-1, keepdims=True))


def mul(left, right):
    return jnp.dot(left, right, preferred_element_type=full_type)


def rows_product(left, right):
    return lax.dot_general(
        left, right, (((0,), (0,)), ((), ())), preferred_element_type=full_type
    )


def times_transpose(left, right):
    return lax.dot_general(
        left, right, (((1,), (1,)), ((), ())), preferred_element_type=full_type
    )


def call(kernel, out_shape, name, **options):
    return pl.pallas_call(
        kernel,
        out_shape=out_shape,
        name=name,
        compiler_params=pltpu.CompilerParams(vmem_limit_bytes=VMEM_LIMIT),
        **options,
    )


def shape(dims, kind):
    return jax.ShapeDtypeStruct(dims, kind)


def route_kernel(
    capacity, order_row, order_col, routes_row, routes_col, slot_row_ref, slot_col_ref
):
    total = order_row.shape[1]
    first, second = routes_col[:, 0:1], routes_col[:, 1:2]
    lane = lax.broadcasted_iota(jnp.int32, (total, LANES), 1)
    picks_first = (first == lane).astype(full_type)
    picks_second = (second == lane).astype(full_type)
    picks = jnp.concatenate([picks_first, picks_second], axis=1).astype(low_type)
    count_first = jnp.sum(picks_first, axis=0, keepdims=True)
    row = lax.broadcasted_iota(jnp.int32, (EXPERTS, total), 0)
    first_row, second_row = routes_row[0:1, :], routes_row[1:2, :]
    across_first = (first_row == row).astype(full_type)
    across_second = (second_row == row).astype(full_type)
    across = jnp.concatenate([across_first, across_second], axis=0).astype(low_type)
    count_across = jnp.sum(across_first, axis=1, keepdims=True)
    bound = jnp.float32(capacity)
    for start in range(0, total, LANES):
        block = pl.ds(start, LANES)
        earlier = (order_row[...] < order_col[block, :]).astype(full_type).astype(low_type)
        counts = mul(earlier, picks)
        mine, other = routes_col[block, 0:1], routes_col[block, 1:2]
        lane_b = lax.broadcasted_iota(jnp.int32, (LANES, LANES), 1)
        slot = jnp.where(
            mine == lane_b,
            counts[:, :LANES],
            jnp.where(other == lane_b, counts[:, LANES:] + count_first, -1.0),
        )
        slot_col_ref[block, :] = jnp.where(slot < bound, slot, -1.0).astype(jnp.int32)
        counts_t = times_transpose(across, earlier)
        row_b = lax.broadcasted_iota(jnp.int32, (EXPERTS, LANES), 0)
        slot_t = jnp.where(
            routes_row[0:1, block] == row_b,
            counts_t[:EXPERTS, :],
            jnp.where(
                routes_row[1:2, block] == row_b, counts_t[EXPERTS:, :] + count_across, -1.0
            ),
        )
        slot_row_ref[:, block] = jnp.where(slot_t < bound, slot_t, -1.0).astype(jnp.int32)


def dispatch_mask(slot_row, slots):
    total = slot_row.shape[-1]
    return lax.broadcasted_iota(jnp.int32, (slots, total), 0) == slot_row


def combine_mask(slot_col, expert, slots):
    total = slot_col.shape[0]
    lane = lax.broadcasted_iota(jnp.int32, (total, LANES), 1)
    mine = jnp.sum(jnp.where(lane == expert, slot_col, 0), axis=1, keepdims=True)
    return lax.broadcasted_iota(jnp.int32, (total, slots), 1) == mine


def as_low(mask):
    return mask.astype(full_type).astype(low_type)


def gather_kernel(slot_row_ref, rows_ref, out_ref):
    mask = dispatch_mask(slot_row_ref[0], out_ref.shape[1])
    out_ref[0] = mul(as_low(mask), rows_ref[...]).astype(low_type)


def side_rows(pack_ref):
    return jnp.transpose(pack_ref[:, SIDE:].astype(full_type))


def experts_kernel(
    slot_row_ref,
    slot_col_ref,
    rows_ref,
    cot_ref,
    up_ref,
    down_ref,
    side_ref,
    rows_out,
    weighted_out,
    grad_pre_out,
    grad_group_out,
    grad_gates_out,
    gates,
    total_acc,
):
    expert = pl.program_id(0)
    slots = cot_ref.shape[1]

    @pl.when(expert == 0)
    def _():
        route_t = side_rows(side_ref)[:EXPERTS].astype(low_type)
        logits = times_transpose(route_t, rows_ref[...])
        raised = jnp.exp(logits - jnp.max(logits, axis=0, keepdims=True))
        gates[...] = raised / jnp.sum(raised, axis=0, keepdims=True)
        total_acc[...] = jnp.zeros_like(total_acc)

    mask = dispatch_mask(slot_row_ref[0], slots)
    expert_in = mul(as_low(mask), rows_ref[...]).astype(low_type)
    gate_row = gates[pl.ds(expert, 1), :]
    weight = jnp.sum(jnp.where(mask, gate_row, 0.0), axis=1, keepdims=True)
    pre = mul(expert_in, up_ref[0])
    grad_hidden = mul(cot_ref[0], down_ref[0])
    slope = math.sqrt(2.0 / math.pi)
    square = pre * pre
    bent = jnp.tanh(slope * (pre + 0.044715 * (pre * square)))
    half = 0.5 * (1.0 + bent)
    hidden = (pre * half).astype(low_type).astype(full_type)
    pull = half + 0.5 * pre * (1.0 - bent * bent) * (slope * (1.0 + (3 * 0.044715) * square))
    grad_weight = jnp.sum(hidden * grad_hidden, axis=1, keepdims=True)
    grad_gates_out[0] = jnp.sum(jnp.where(mask, grad_weight, 0.0), axis=0, keepdims=True)
    grad_pre = (weight * grad_hidden * pull).astype(low_type)
    rows_out[0] = expert_in
    weighted_out[0] = (weight * hidden).astype(low_type)
    grad_pre_out[0] = grad_pre
    grad_in = times_transpose(grad_pre, up_ref[0]).astype(low_type)
    back = as_low(combine_mask(slot_col_ref[...], expert, slots))
    total_acc[...] += mul(back, grad_in)

    @pl.when(expert == EXPERTS - 1)
    def _():
        grad_group_out[...] = total_acc[...].astype(low_type)


def weights_kernel(rows_ref, cot_ref, weighted_ref, grad_pre_ref, out_ref):
    out_ref[0, 0] = rows_product(rows_ref[0], grad_pre_ref[0]).astype(low_type)
    out_ref[0, 1] = rows_product(cot_ref[0], weighted_ref[0]).astype(low_type)


def combine_kernel(slot_col_ref, weighted_ref, down_ref, out_ref, total_acc):
    expert = pl.program_id(0)

    @pl.when(expert == 0)
    def _():
        total_acc[...] = jnp.zeros_like(total_acc)

    expert_out = times_transpose(weighted_ref[0], down_ref[0]).astype(low_type)
    back = as_low(combine_mask(slot_col_ref[...], expert, weighted_ref.shape[1]))
    total_acc[...] += mul(back, expert_out)

    @pl.when(expert == EXPERTS - 1)
    def _():
        out_ref[...] = total_acc[...].astype(low_type)


def head_masks():
    lane = lax.broadcasted_iota(jnp.int32, (1, LANES), 1)
    left = (lane < HEAD).astype(full_type).astype(low_type)
    return (left, 1.0 - left)


def softmax_rows(queries, keys):
    scores = times_transpose(queries, keys) * (1.0 / math.sqrt(HEAD))
    column = lax.broadcasted_iota(jnp.int32, scores.shape, 1)
    scores = jnp.where(column < SEQ, scores, -1e30)
    raised = jnp.exp(scores - jnp.max(scores, axis=-1, keepdims=True))
    return raised / jnp.sum(raised, axis=-1, keepdims=True)


def head_pairs(images):
    for image in range(images):
        rows = pl.ds(image * ROWS, ROWS)
        for pair in range(HEADS * HEAD // LANES):
            yield rows, tuple(
                pl.ds(part * D + pair * LANES, LANES) for part in range(3)
            )


def forward_kernel(tokens_ref, pack_ref, a_two_ref, y_ref, proj_ref, context_ref):
    side = side_rows(pack_ref)
    values = tokens_ref[...].astype(full_type)
    images = tokens_ref.shape[0] // ROWS
    normed, _ = norm_forward(values)
    a_one = (normed * side[8:9] + side[9:10]).astype(low_type)
    proj_ref[...] = mul(a_one, pack_ref[:, : 3 * D]).astype(low_type)
    masks = head_masks()
    lane = lax.broadcasted_iota(jnp.int32, (ROWS, LANES), 1)
    for rows, (q_at, k_at, v_at) in head_pairs(images):
        queries, keys, vals = proj_ref[rows, q_at], proj_ref[rows, k_at], proj_ref[rows, v_at]
        both = [
            mul(softmax_rows(queries * mask, keys).astype(low_type), vals) for mask in masks
        ]
        context_ref[rows, q_at] = jnp.where(lane < HEAD, both[0], both[1]).astype(low_type)
    y_one = values + mul(context_ref[...], pack_ref[:, 3 * D : SIDE])
    y_ref[...] = y_one
    normed_two, _ = norm_forward(y_one)
    a_two_ref[...] = (normed_two * side[10:11] + side[11:12]).astype(low_type)


def backward_kernel(
    grad_moe_ref,
    grad_gates_ref,
    a_two_ref,
    y_ref,
    cot_ref,
    context_ref,
    proj_ref,
    tokens_ref,
    pack_ref,
    grad_tokens_ref,
    grad_pack_ref,
    grad_proj,
    grad_context,
):
    side = side_rows(pack_ref)
    gain_a, offset_a, gain_b = side[8:9], side[9:10], side[10:11]
    route_t = side[:EXPERTS].astype(low_type)
    a_two = a_two_ref[...]
    images = a_two.shape[0] // ROWS
    logits = times_transpose(route_t, a_two)
    raised = jnp.exp(logits - jnp.max(logits, axis=0, keepdims=True))
    gates = raised / jnp.sum(raised, axis=0, keepdims=True)
    grad_gates = jnp.sum(grad_gates_ref[...], axis=0)
    grad_logits = (
        gates * (grad_gates - jnp.sum(gates * grad_gates, axis=0, keepdims=True))
    ).astype(low_type)
    grad_route = mul(grad_logits, a_two)
    grad_a_two = grad_moe_ref[0].astype(full_type)
    for part in range(1, grad_moe_ref.shape[0]):
        grad_a_two += grad_moe_ref[part].astype(full_type)
    grad_a_two += rows_product(grad_logits, route_t)
    normed_two, inv_two = norm_forward(y_ref[...])
    grad_gain_b = jnp.sum(grad_a_two * normed_two, axis=0, keepdims=True)
    grad_offset_b = jnp.sum(grad_a_two, axis=0, keepdims=True)
    grad_y = cot_ref[...].astype(full_type) + norm_backward(
        grad_a_two, normed_two, inv_two, gain_b
    )
    grad_branch = grad_y.astype(low_type)
    grad_pack_ref[:, 3 * D : SIDE] = rows_product(context_ref[...], grad_branch).astype(low_type)
    grad_context[...] = times_transpose(grad_branch, pack_ref[:, 3 * D : SIDE]).astype(low_type)
    masks = head_masks()
    scale = 1.0 / math.sqrt(HEAD)
    for rows, (q_at, k_at, v_at) in head_pairs(images):
        queries, keys, vals = proj_ref[rows, q_at], proj_ref[rows, k_at], proj_ref[rows, v_at]
        grads = grad_context[rows, q_at]
        grad_q, grad_k, grad_v = 0.0, 0.0, 0.0
        for mask in masks:
            own_q, own_k, own_g = queries * mask, keys * mask, grads * mask
            probs = softmax_rows(own_q, keys)
            grad_probs = times_transpose(own_g, vals)
            dots = jnp.sum(probs * grad_probs, axis=-1, keepdims=True)
            grad_scores = (probs * (grad_probs - dots)).astype(low_type)
            grad_v += rows_product(probs.astype(low_type), own_g)
            grad_q += mul(grad_scores, own_k)
            grad_k += rows_product(grad_scores, own_q)
        grad_proj[rows, q_at] = (grad_q * scale).astype(low_type)
        grad_proj[rows, k_at] = (grad_k * scale).astype(low_type)
        grad_proj[rows, v_at] = grad_v.astype(low_type)
    values = tokens_ref[...].astype(full_type)
    normed_one, inv_one = norm_forward(values)
    a_one = (normed_one * gain_a + offset_a).astype(low_type)
    grad_pack_ref[:, : 3 * D] = rows_product(a_one, grad_proj[...]).astype(low_type)
    grad_a_one = times_transpose(grad_proj[...], pack_ref[:, : 3 * D])
    grad_gain_a = jnp.sum(grad_a_one * normed_one, axis=0, keepdims=True)
    grad_offset_a = jnp.sum(grad_a_one, axis=0, keepdims=True)
    grad_tokens_ref[...] = (
        grad_y + norm_backward(grad_a_one, normed_one, inv_one, gain_a)
    ).astype(low_type)
    row = lax.broadcasted_iota(jnp.int32, (EXPERTS, D), 0)
    norms = jnp.where(
        row == 0,
        grad_gain_a,
        jnp.where(
            row == 1,
            grad_offset_a,
            jnp.where(row == 2, grad_gain_b, jnp.where(row == 3, grad_offset_b, 0.0)),
        ),
    )
    spare = jnp.zeros((LANES - 2 * EXPERTS, D), full_type)
    sides = jnp.concatenate([grad_route, norms, spare], axis=0)
    grad_pack_ref[:, SIDE:] = jnp.transpose(sides).astype(low_type)


def pad_images(rows):
    width = rows.shape[-1]
    images = rows.shape[0] // SEQ
    apart = rows.reshape(images, SEQ, width)
    return jnp.pad(apart, ((0, 0), (0, ROWS - SEQ), (0, 0))).reshape(images * ROWS, width)


def drop_padding(rows):
    width = rows.shape[-1]
    images = rows.shape[0] // ROWS
    return rows.reshape(images, ROWS, width)[:, :SEQ].reshape(images * SEQ, width)


def swap(blocks, axis_name):
    return lax.all_to_all(blocks, axis_name, 0, 0, tiled=True)


def add_up(blocks, axis_name):
    return jnp.sum(swap(blocks, axis_name).astype(full_type), axis=0)


def gather_pack(pack):
    wide = lax.all_gather(pack, "tp", axis=0, tiled=True)
    return lax.all_gather(wide, ROW_AXES, axis=0, tiled=True)


def reduce_pack(grad_pack):
    sizes = tuple(lax.axis_size(name) for name in ALL_AXES)
    own = grad_pack.shape[0] // math.prod(sizes)
    rest = (own, grad_pack.shape[1])
    blocks = grad_pack.reshape(sizes + rest)
    blocks = add_up(jnp.moveaxis(blocks, 1, 0), "ctx").astype(low_type)
    blocks = add_up(jnp.moveaxis(blocks, 1, 0), "tp").astype(low_type)
    return add_up(blocks, "fsdp")


def on_device(
    tokens,
    w_qkv,
    w_attend,
    w_route,
    gain_one,
    shift_one,
    gain_two,
    shift_two,
    w_up,
    w_down,
    routes,
    priority,
    cotangent,
):
    tok_rows = tokens.shape[0]
    tp_size = lax.axis_size("tp")
    images = tok_rows // SEQ
    own_rows = images * ROWS
    group_rows = tok_rows * tp_size
    total = own_rows * tp_size
    capacity = group_rows * TOP * 5 // (4 * EXPERTS)
    slots = -(-capacity // 16) * 16
    hidden_width = w_up.shape[2]

    columns = [w_qkv, w_attend, w_route]
    columns += [v[:, None] for v in (gain_one, shift_one, gain_two, shift_two)]
    pack = jnp.concatenate(columns, axis=1).astype(low_type)
    pack = jnp.pad(pack, ((0, 0), (0, WIDE - pack.shape[1])))
    pack_all = gather_pack(pack)

    cot_pad = pad_images(cotangent)
    tok_pad = pad_images(tokens)
    cot_group = lax.all_gather(cot_pad, "tp", axis=0, tiled=True)
    both = jnp.stack([w_up, w_down]).astype(low_type)
    both_all = lax.all_gather(both, ROW_AXES, axis=2, tiled=True)
    up_w, down_w = both_all[0], both_all[1]

    spread = jnp.pad(
        jnp.concatenate([routes, priority.reshape(-1, 1)], axis=1).reshape(
            group_rows // SEQ, SEQ, TOP + 1
        ),
        ((0, 0), (0, ROWS - SEQ), (0, 0)),
        constant_values=-1,
    ).reshape(total, TOP + 1)
    spread_t = spread.T
    slot_row, slot_col = call(
        partial(route_kernel, capacity),
        (shape((EXPERTS, total), jnp.int32), shape((total, LANES), jnp.int32)),
        "route",
    )(spread_t[TOP:], spread[:, TOP:], spread_t[:TOP], spread[:, :TOP])
    slot_row = slot_row.reshape(EXPERTS, 1, total)

    a_two, y_one, proj, context = call(
        forward_kernel,
        (
            shape((own_rows, D), low_type),
            shape((own_rows, D), full_type),
            shape((own_rows, 3 * D), low_type),
            shape((own_rows, D), low_type),
        ),
        "attend_forward",
    )(tok_pad, pack_all)

    a_group = lax.all_gather(a_two, "tp", axis=0, tiled=True)

    slot_row_spec = pl.BlockSpec((1, 1, total), lambda e: (e, 0, 0))
    slot_col_spec = pl.BlockSpec((total, LANES), lambda e: (0, 0))
    group_spec = pl.BlockSpec((total, D), lambda e: (0, 0))
    in_spec = pl.BlockSpec((1, slots, D), lambda e: (e, 0, 0))
    mid_spec = pl.BlockSpec((1, slots, hidden_width), lambda e: (e, 0, 0))
    weight_spec = pl.BlockSpec((1, D, hidden_width), lambda e: (e, 0, 0))
    pack_spec = pl.BlockSpec((D, WIDE), lambda e: (0, 0))

    cot_slots = call(
        gather_kernel,
        shape((EXPERTS, slots, D), low_type),
        "gather_cotangent",
        grid=(EXPERTS,),
        in_specs=[slot_row_spec, group_spec],
        out_specs=in_spec,
    )(slot_row, cot_group)

    expert_in, weighted, grad_pre, grad_group, grad_gates = call(
        experts_kernel,
        (
            shape((EXPERTS, slots, D), low_type),
            shape((EXPERTS, slots, hidden_width), low_type),
            shape((EXPERTS, slots, hidden_width), low_type),
            shape((total, D), low_type),
            shape((EXPERTS, 1, total), full_type),
        ),
        "experts",
        grid=(EXPERTS,),
        in_specs=[
            slot_row_spec,
            slot_col_spec,
            group_spec,
            in_spec,
            weight_spec,
            weight_spec,
            pack_spec,
        ],
        out_specs=(in_spec, mid_spec, mid_spec, group_spec, slot_row_spec),
        scratch_shapes=[
            pltpu.VMEM((EXPERTS, total), full_type),
            pltpu.VMEM((total, D), full_type),
        ],
    )(slot_row, slot_col, a_group, cot_slots, up_w, down_w, pack_all)

    grad_moe = swap(grad_group.reshape(tp_size, own_rows, D), "tp")
    gates_blocks = jnp.moveaxis(grad_gates.reshape(EXPERTS, tp_size, own_rows), 1, 0)
    grad_gates_own = swap(gates_blocks, "tp")

    grad_both = call(
        weights_kernel,
        shape((EXPERTS, 2, D, hidden_width), low_type),
        "expert_weights",
        grid=(EXPERTS,),
        in_specs=[in_spec, in_spec, mid_spec, mid_spec],
        out_specs=pl.BlockSpec((1, 2, D, hidden_width), lambda e: (e, 0, 0, 0)),
    )(expert_in, cot_slots, weighted, grad_pre)
    grad_both = lax.psum_scatter(grad_both, ROW_AXES, scatter_dimension=2, tiled=True)

    combined = call(
        combine_kernel,
        shape((total, D), low_type),
        "combine",
        grid=(EXPERTS,),
        in_specs=[slot_col_spec, mid_spec, weight_spec],
        out_specs=group_spec,
        scratch_shapes=[pltpu.VMEM((total, D), full_type)],
    )(slot_col, weighted, down_w)

    grad_tokens, grad_pack = call(
        backward_kernel,
        (shape((own_rows, D), low_type), shape((D, WIDE), low_type)),
        "attend_backward",
        scratch_shapes=[
            pltpu.VMEM((own_rows, 3 * D), low_type),
            pltpu.VMEM((own_rows, D), low_type),
        ],
    )(grad_moe, grad_gates_own, a_two, y_one, cot_pad, context, proj, tok_pad, pack_all)

    moe_rows = add_up(combined.reshape(tp_size, own_rows, D), "tp")
    output = drop_padding((y_one + moe_rows).astype(low_type))
    reduced = reduce_pack(grad_pack)
    grad_both = grad_both.astype(full_type)
    return (
        output,
        drop_padding(grad_tokens),
        reduced[:, : 3 * D],
        reduced[:, 3 * D : SIDE],
        reduced[:, SIDE : SIDE + EXPERTS],
        reduced[:, SIDE + 8],
        reduced[:, SIDE + 9],
        reduced[:, SIDE + 10],
        reduced[:, SIDE + 11],
        grad_both[:, 0],
        grad_both[:, 1],
    )


def solution(mesh):
    rows = P(ALL_AXES, None)
    vector = P(ALL_AXES)
    weights = P(None, ROW_AXES, "tp")
    group = P(ROW_AXES, None)
    in_specs = (rows,) * 4 + (vector,) * 4 + (weights,) * 2 + (group,) * 2 + (rows,)
    out_specs = (rows,) * 5 + (vector,) * 4 + (weights,) * 2
    return jax.shard_map(
        on_device, mesh=mesh, in_specs=in_specs, out_specs=out_specs, check_vma=False
    )
```

```python
from functools import partial
import math

import jax
import jax.numpy as jnp
from jax import lax
from jax.experimental import pallas as pl
from jax.experimental.pallas import tpu as pltpu
from jax.sharding import PartitionSpec as P

D = 512
HEADS = 8
HEAD = 64
SEQ = 197
TOP = 2
EXPERTS = 8

LANES = 128
ROWS = 208
WIDE = 3 * D + D + LANES
SIDE = 4 * D

epsilon = 1e-06
low_type = jnp.bfloat16
full_type = jnp.float32
ALL_AXES = ("fsdp", "ctx", "tp")
ROW_AXES = ("fsdp", "ctx")
VMEM_LIMIT = 58 * 1024 * 1024


def norm_forward(values):
    center = values - jnp.mean(values, axis=-1, keepdims=True)
    spread = jnp.mean(center * center, axis=-1, keepdims=True)
    inv_scale = lax.rsqrt(spread + epsilon)
    return (center * inv_scale, inv_scale)


def norm_backward(grad_norm, normed, inv_scale, gain_row):
    scaled = grad_norm * gain_row
    centred = scaled - jnp.mean(scaled, axis=-1, keepdims=True)
    return inv_scale * (centred - normed * jnp.mean(scaled * normed, axis=-1, keepdims=True))


def mul(left, right):
    return jnp.dot(left, right, preferred_element_type=full_type)


def rows_product(left, right):
    return lax.dot_general(
        left, right, (((0,), (0,)), ((), ())), preferred_element_type=full_type
    )


def times_transpose(left, right):
    return lax.dot_general(
        left, right, (((1,), (1,)), ((), ())), preferred_element_type=full_type
    )


def call(kernel, out_shape, name, **options):
    return pl.pallas_call(
        kernel,
        out_shape=out_shape,
        name=name,
        compiler_params=pltpu.CompilerParams(vmem_limit_bytes=VMEM_LIMIT),
        **options,
    )


def shape(dims, kind):
    return jax.ShapeDtypeStruct(dims, kind)


def route_kernel(
    capacity, order_row, order_col, routes_row, routes_col, slot_row_ref, slot_col_ref
):
    total = order_row.shape[1]
    first, second = routes_col[:, 0:1], routes_col[:, 1:2]
    lane = lax.broadcasted_iota(jnp.int32, (total, LANES), 1)
    picks_first = (first == lane).astype(full_type)
    picks_second = (second == lane).astype(full_type)
    picks = jnp.concatenate([picks_first, picks_second], axis=1).astype(low_type)
    count_first = jnp.sum(picks_first, axis=0, keepdims=True)
    row = lax.broadcasted_iota(jnp.int32, (EXPERTS, total), 0)
    first_row, second_row = routes_row[0:1, :], routes_row[1:2, :]
    across_first = (first_row == row).astype(full_type)
    across_second = (second_row == row).astype(full_type)
    across = jnp.concatenate([across_first, across_second], axis=0).astype(low_type)
    count_across = jnp.sum(across_first, axis=1, keepdims=True)
    bound = jnp.float32(capacity)
    for start in range(0, total, LANES):
        block = pl.ds(start, LANES)
        earlier = (order_row[...] < order_col[block, :]).astype(full_type).astype(low_type)
        counts = mul(earlier, picks)
        mine, other = routes_col[block, 0:1], routes_col[block, 1:2]
        lane_b = lax.broadcasted_iota(jnp.int32, (LANES, LANES), 1)
        slot = jnp.where(
            mine == lane_b,
            counts[:, :LANES],
            jnp.where(other == lane_b, counts[:, LANES:] + count_first, -1.0),
        )
        slot_col_ref[block, :] = jnp.where(slot < bound, slot, -1.0).astype(jnp.int32)
        counts_t = times_transpose(across, earlier)
        row_b = lax.broadcasted_iota(jnp.int32, (EXPERTS, LANES), 0)
        slot_t = jnp.where(
            routes_row[0:1, block] == row_b,
            counts_t[:EXPERTS, :],
            jnp.where(
                routes_row[1:2, block] == row_b, counts_t[EXPERTS:, :] + count_across, -1.0
            ),
        )
        slot_row_ref[:, block] = jnp.where(slot_t < bound, slot_t, -1.0).astype(jnp.int32)


def dispatch_mask(slot_row, slots):
    total = slot_row.shape[-1]
    return lax.broadcasted_iota(jnp.int32, (slots, total), 0) == slot_row


def combine_mask(slot_col, expert, slots):
    total = slot_col.shape[0]
    lane = lax.broadcasted_iota(jnp.int32, (total, LANES), 1)
    mine = jnp.sum(jnp.where(lane == expert, slot_col, 0), axis=1, keepdims=True)
    return lax.broadcasted_iota(jnp.int32, (total, slots), 1) == mine


def as_low(mask):
    return mask.astype(full_type).astype(low_type)


def join_parts(part_refs, whole):
    own = part_refs[0].shape[0]
    for index, part in enumerate(part_refs):
        whole[index * own : (index + 1) * own, :] = part[...]


def gather_kernel(parts, slot_row_ref, *refs):
    part_refs, (out_ref, whole) = refs[:parts], refs[parts:]

    @pl.when(pl.program_id(0) == 0)
    def _():
        join_parts(part_refs, whole)

    mask = dispatch_mask(slot_row_ref[0], out_ref.shape[1])
    out_ref[0] = mul(as_low(mask), whole[...]).astype(low_type)


def side_rows(pack_ref):
    return jnp.transpose(pack_ref[:, SIDE:].astype(full_type))


def experts_kernel(parts, slot_row_ref, slot_col_ref, cot_ref, up_ref, down_ref, side_ref, *refs):
    part_refs, refs = refs[:parts], refs[parts:]
    (rows_out, weighted_out, grad_pre_out), refs = refs[:3], refs[3:]
    group_outs, (rows_ref, gates, grad_gates, total_acc) = refs[:parts], refs[parts:]
    expert = pl.program_id(0)
    slots = cot_ref.shape[1]

    @pl.when(expert == 0)
    def _():
        join_parts(part_refs, rows_ref)
        route_t = side_rows(side_ref)[:EXPERTS].astype(low_type)
        logits = times_transpose(route_t, rows_ref[...])
        raised = jnp.exp(logits - jnp.max(logits, axis=0, keepdims=True))
        gates[...] = raised / jnp.sum(raised, axis=0, keepdims=True)
        total_acc[...] = jnp.zeros_like(total_acc)

    mask = dispatch_mask(slot_row_ref[0], slots)
    expert_in = mul(as_low(mask), rows_ref[...]).astype(low_type)
    gate_row = gates[pl.ds(expert, 1), :]
    weight = jnp.sum(jnp.where(mask, gate_row, 0.0), axis=1, keepdims=True)
    pre = mul(expert_in, up_ref[0, 0])
    grad_hidden = mul(cot_ref[0], down_ref[0, 0])
    slope = math.sqrt(2.0 / math.pi)
    square = pre * pre
    bent = jnp.tanh(slope * (pre + 0.044715 * (pre * square)))
    half = 0.5 * (1.0 + bent)
    hidden = (pre * half).astype(low_type).astype(full_type)
    pull = half + 0.5 * pre * (1.0 - bent * bent) * (slope * (1.0 + (3 * 0.044715) * square))
    grad_weight = jnp.sum(hidden * grad_hidden, axis=1, keepdims=True)
    grad_gates[pl.ds(expert, 1), :] = jnp.sum(
        jnp.where(mask, grad_weight, 0.0), axis=0, keepdims=True
    )
    grad_pre = (weight * grad_hidden * pull).astype(low_type)
    rows_out[0] = expert_in
    weighted_out[0] = (weight * hidden).astype(low_type)
    grad_pre_out[0] = grad_pre
    grad_in = times_transpose(grad_pre, up_ref[0, 0]).astype(low_type)
    back = as_low(combine_mask(slot_col_ref[...], expert, slots))
    total_acc[...] += mul(back, grad_in)

    @pl.when(expert == EXPERTS - 1)
    def _():
        own = part_refs[0].shape[0]
        total = rows_ref.shape[0]
        for index, out in enumerate(group_outs):
            out[:own, :] = total_acc[index * own : (index + 1) * own, :].astype(low_type)
            gates_part = pltpu.roll(grad_gates[...], (total - index * own) % total, 1)[:, :D]
            high = gates_part.astype(low_type).astype(full_type)
            pair = jnp.concatenate([high, gates_part - high], axis=0)
            out[own:, :] = pair.astype(low_type)


def weights_kernel(rows_ref, cot_ref, weighted_ref, grad_pre_ref, out_ref):
    out_ref[0, 0] = rows_product(rows_ref[0], grad_pre_ref[0]).astype(low_type)
    out_ref[0, 1] = rows_product(cot_ref[0], weighted_ref[0]).astype(low_type)


def combine_kernel(slot_col_ref, weighted_ref, down_ref, *refs):
    outs, total_acc = refs[:-1], refs[-1]
    expert = pl.program_id(0)

    @pl.when(expert == 0)
    def _():
        total_acc[...] = jnp.zeros_like(total_acc)

    expert_out = times_transpose(weighted_ref[0], down_ref[0, 0]).astype(low_type)
    back = as_low(combine_mask(slot_col_ref[...], expert, weighted_ref.shape[1]))
    total_acc[...] += mul(back, expert_out)

    @pl.when(expert == EXPERTS - 1)
    def _():
        own = outs[0].shape[0]
        for index, out in enumerate(outs):
            out[...] = total_acc[index * own : (index + 1) * own, :].astype(low_type)


def head_masks():
    lane = lax.broadcasted_iota(jnp.int32, (1, LANES), 1)
    left = (lane < HEAD).astype(full_type).astype(low_type)
    return (left, 1.0 - left)


def softmax_rows(queries, keys):
    scores = times_transpose(queries, keys) * (1.0 / math.sqrt(HEAD))
    column = lax.broadcasted_iota(jnp.int32, scores.shape, 1)
    scores = jnp.where(column < SEQ, scores, -1e30)
    raised = jnp.exp(scores - jnp.max(scores, axis=-1, keepdims=True))
    return raised / jnp.sum(raised, axis=-1, keepdims=True)


def head_pairs(images):
    for image in range(images):
        rows = pl.ds(image * ROWS, ROWS)
        for pair in range(HEADS * HEAD // LANES):
            yield rows, tuple(
                pl.ds(part * D + pair * LANES, LANES) for part in range(3)
            )


def forward_kernel(places, block, offset_ref, tokens_ref, *refs):
    pieces, (a_two_ref, y_ref, proj_ref, context_ref, pack_ref) = refs[:-5], refs[-5:]
    for piece, place in zip(pieces, places):
        for index, at in enumerate(place):
            start = pl.multiple_of(offset_ref[at], block)
            pack_ref[pl.ds(start, block), :] = piece[index * block : (index + 1) * block, :]
    side = side_rows(pack_ref)
    values = tokens_ref[...].astype(full_type)
    images = tokens_ref.shape[0] // ROWS
    normed, _ = norm_forward(values)
    a_one = (normed * side[8:9] + side[9:10]).astype(low_type)
    proj_ref[...] = mul(a_one, pack_ref[:, : 3 * D]).astype(low_type)
    masks = head_masks()
    lane = lax.broadcasted_iota(jnp.int32, (ROWS, LANES), 1)
    for rows, (q_at, k_at, v_at) in head_pairs(images):
        queries, keys, vals = proj_ref[rows, q_at], proj_ref[rows, k_at], proj_ref[rows, v_at]
        both = [
            mul(softmax_rows(queries * mask, keys).astype(low_type), vals) for mask in masks
        ]
        context_ref[rows, q_at] = jnp.where(lane < HEAD, both[0], both[1]).astype(low_type)
    y_one = values + mul(context_ref[...], pack_ref[:, 3 * D : SIDE])
    y_ref[...] = y_one
    normed_two, _ = norm_forward(y_one)
    a_two_ref[...] = (normed_two * side[10:11] + side[11:12]).astype(low_type)


def backward_kernel(
    parts,
    block,
    offset_ref,
    a_two_ref,
    y_ref,
    cot_ref,
    context_ref,
    proj_ref,
    tokens_ref,
    pack_ref,
    *refs,
):
    grad_refs, grad_tokens_ref, outs = refs[:parts], refs[parts], refs[parts + 1 : -3]
    grad_pack_ref, grad_proj, grad_context = refs[-3:]
    side = side_rows(pack_ref)
    gain_a, offset_a, gain_b = side[8:9], side[9:10], side[10:11]
    route_t = side[:EXPERTS].astype(low_type)
    a_two = a_two_ref[...]
    images = a_two.shape[0] // ROWS
    logits = times_transpose(route_t, a_two)
    raised = jnp.exp(logits - jnp.max(logits, axis=0, keepdims=True))
    gates = raised / jnp.sum(raised, axis=0, keepdims=True)
    own = a_two.shape[0]
    arrived = grad_refs[0][...].astype(full_type)
    for part in grad_refs[1:]:
        arrived += part[...].astype(full_type)
    grad_gates = arrived[own : own + EXPERTS, :own] + arrived[own + EXPERTS :, :own]
    grad_logits = (
        gates * (grad_gates - jnp.sum(gates * grad_gates, axis=0, keepdims=True))
    ).astype(low_type)
    grad_route = mul(grad_logits, a_two)
    grad_a_two = arrived[:own] + rows_product(grad_logits, route_t)
    normed_two, inv_two = norm_forward(y_ref[...])
    grad_gain_b = jnp.sum(grad_a_two * normed_two, axis=0, keepdims=True)
    grad_offset_b = jnp.sum(grad_a_two, axis=0, keepdims=True)
    grad_y = cot_ref[...].astype(full_type) + norm_backward(
        grad_a_two, normed_two, inv_two, gain_b
    )
    grad_branch = grad_y.astype(low_type)
    grad_pack_ref[:, 3 * D : SIDE] = rows_product(context_ref[...], grad_branch).astype(low_type)
    grad_context[...] = times_transpose(grad_branch, pack_ref[:, 3 * D : SIDE]).astype(low_type)
    masks = head_masks()
    scale = 1.0 / math.sqrt(HEAD)
    for rows, (q_at, k_at, v_at) in head_pairs(images):
        queries, keys, vals = proj_ref[rows, q_at], proj_ref[rows, k_at], proj_ref[rows, v_at]
        grads = grad_context[rows, q_at]
        grad_q, grad_k, grad_v = 0.0, 0.0, 0.0
        for mask in masks:
            own_q, own_k, own_g = queries * mask, keys * mask, grads * mask
            probs = softmax_rows(own_q, keys)
            grad_probs = times_transpose(own_g, vals)
            dots = jnp.sum(probs * grad_probs, axis=-1, keepdims=True)
            grad_scores = (probs * (grad_probs - dots)).astype(low_type)
            grad_v += rows_product(probs.astype(low_type), own_g)
            grad_q += mul(grad_scores, own_k)
            grad_k += rows_product(grad_scores, own_q)
        grad_proj[rows, q_at] = (grad_q * scale).astype(low_type)
        grad_proj[rows, k_at] = (grad_k * scale).astype(low_type)
        grad_proj[rows, v_at] = grad_v.astype(low_type)
    values = tokens_ref[...].astype(full_type)
    normed_one, inv_one = norm_forward(values)
    a_one = (normed_one * gain_a + offset_a).astype(low_type)
    grad_pack_ref[:, : 3 * D] = rows_product(a_one, grad_proj[...]).astype(low_type)
    grad_a_one = times_transpose(grad_proj[...], pack_ref[:, : 3 * D])
    grad_gain_a = jnp.sum(grad_a_one * normed_one, axis=0, keepdims=True)
    grad_offset_a = jnp.sum(grad_a_one, axis=0, keepdims=True)
    grad_tokens_ref[...] = (
        grad_y + norm_backward(grad_a_one, normed_one, inv_one, gain_a)
    ).astype(low_type)
    row = lax.broadcasted_iota(jnp.int32, (EXPERTS, D), 0)
    norms = jnp.where(
        row == 0,
        grad_gain_a,
        jnp.where(
            row == 1,
            grad_offset_a,
            jnp.where(row == 2, grad_gain_b, jnp.where(row == 3, grad_offset_b, 0.0)),
        ),
    )
    spare = jnp.zeros((LANES - 2 * EXPERTS, D), full_type)
    sides = jnp.concatenate([grad_route, norms, spare], axis=0)
    grad_pack_ref[:, SIDE:] = jnp.transpose(sides).astype(low_type)
    at = 0
    for out in outs:
        for index in range(out.shape[0] // block):
            start = pl.multiple_of(offset_ref[at], block)
            out[index * block : (index + 1) * block, :] = grad_pack_ref[pl.ds(start, block), :]
            at += 1


def pad_images(rows):
    width = rows.shape[-1]
    images = rows.shape[0] // SEQ
    apart = rows.reshape(images, SEQ, width)
    return jnp.pad(apart, ((0, 0), (0, ROWS - SEQ), (0, 0))).reshape(images * ROWS, width)


def drop_padding(rows):
    width = rows.shape[-1]
    images = rows.shape[0] // ROWS
    return rows.reshape(images, ROWS, width)[:, :SEQ].reshape(images * SEQ, width)


def swap(blocks, axis_name):
    return lax.all_to_all(blocks, axis_name, 0, 0, tiled=True)


def add_up(blocks, axis_name):
    return jnp.sum(swap(blocks, axis_name).astype(full_type), axis=0)


def rotate(value, axis_name, step):
    size = lax.axis_size(axis_name)
    return lax.ppermute(value, axis_name, [(i, (i + step) % size) for i in range(size)])


def cross(value, axis_name, bit):
    size = lax.axis_size(axis_name)
    return lax.ppermute(value, axis_name, [(i, i ^ bit) for i in range(size)])


def collect(part):
    return [part] + [rotate(part, "tp", step) for step in range(1, lax.axis_size("tp"))]


def deliver(parts):
    return [parts[0]] + [rotate(part, "tp", -step) for step, part in enumerate(parts) if step]


def near_mesh():
    return lax.axis_size("fsdp") == 2 and lax.axis_size("ctx") == 4 and lax.axis_size("tp") == 4


def pack_offsets(block):
    spot = jnp.arange(32, dtype=jnp.int32)
    core, y, x, back = spot // 16, spot // 8 % 2, spot // 4 % 2, spot % 4
    row = (lax.axis_index("fsdp") ^ y) * 4 + (lax.axis_index("ctx") ^ (2 * x + core))
    return ((row * 4 + (lax.axis_index("tp") - back + 4) % 4) * block).astype(jnp.int32)


def gather_near(pack):
    column = jnp.concatenate(collect(pack), axis=0)
    half = column.shape[0] // 2
    over_x, over_y = cross(column, "ctx", 2), cross(column, "fsdp", 1)
    low_half = cross(over_y[:half], "ctx", 2)
    high_half = cross(over_x[half:], "fsdp", 1)
    pieces = [column, over_x, over_y, low_half, high_half]
    pieces += [cross(piece, "ctx", 1) for piece in pieces]
    places = [range(0, 4), range(4, 8), range(8, 12), range(12, 14), range(14, 16)]
    places += [[spot + 16 for spot in place] for place in places]
    return pieces, [list(place) for place in places]


def add_low(left, right):
    return (left.astype(full_type) + right.astype(full_type)).astype(low_type)


def reduce_near(own, other):
    rest = (own.shape[0] // 16, own.shape[1])
    sums = add_low(own, cross(other, "ctx", 1)).reshape((2, 2, 4) + rest)
    far = sums[1, 1]
    by_x, by_y = cross(far[:2], "ctx", 2), cross(far[2:], "fsdp", 1)
    to_y = jnp.concatenate([add_low(sums[1, 0, :2], by_x), sums[1, 0, 2:]], axis=0)
    to_x = jnp.concatenate([sums[0, 1, :2], add_low(sums[0, 1, 2:], by_y)], axis=0)
    column = add_low(add_low(sums[0, 0], cross(to_x, "ctx", 2)), cross(to_y, "fsdp", 1))
    arrived = deliver([column[step] for step in range(4)])
    return sum(part.astype(full_type) for part in arrived)


def gather_far(pack):
    wide = lax.all_gather(pack, "tp", axis=0, tiled=True)
    return [lax.all_gather(wide, ROW_AXES, axis=0, tiled=True)], [[0]]


def reduce_far(grad_pack):
    sizes = tuple(lax.axis_size(name) for name in ALL_AXES)
    own = grad_pack.shape[0] // math.prod(sizes)
    rest = (own, grad_pack.shape[1])
    blocks = grad_pack.reshape(sizes + rest)
    blocks = add_up(jnp.moveaxis(blocks, 1, 0), "ctx").astype(low_type)
    blocks = add_up(jnp.moveaxis(blocks, 1, 0), "tp").astype(low_type)
    return add_up(blocks, "fsdp")


def on_device(
    tokens,
    w_qkv,
    w_attend,
    w_route,
    gain_one,
    shift_one,
    gain_two,
    shift_two,
    w_up,
    w_down,
    routes,
    priority,
    cotangent,
):
    tok_rows = tokens.shape[0]
    tp_size = lax.axis_size("tp")
    images = tok_rows // SEQ
    own_rows = images * ROWS
    group_rows = tok_rows * tp_size
    total = own_rows * tp_size
    capacity = group_rows * TOP * 5 // (4 * EXPERTS)
    slots = -(-capacity // 16) * 16
    hidden_width = w_up.shape[2]

    columns = [w_qkv, w_attend, w_route]
    columns += [v[:, None] for v in (gain_one, shift_one, gain_two, shift_two)]
    pack = jnp.concatenate(columns, axis=1).astype(low_type)
    pack = jnp.pad(pack, ((0, 0), (0, WIDE - pack.shape[1])))
    near = near_mesh()
    if near:
        block = pack.shape[0]
        offsets = pack_offsets(block)
        pieces, places = gather_near(pack)
        half = D // 2
        grad_shapes = [shape((half, WIDE), low_type)] * 2
    else:
        block = D
        offsets = jnp.zeros((1,), jnp.int32)
        pieces, places = gather_far(pack)
        grad_shapes = [shape((D, WIDE), low_type)]

    cotangent, first_piece = lax.optimization_barrier((cotangent, pieces[0]))
    pieces[0] = first_piece
    cot_pad = pad_images(cotangent)
    tok_pad = pad_images(tokens)
    cot_parts = collect(cot_pad)
    both = jnp.stack([w_up, w_down]).astype(low_type)
    both_all = lax.all_gather(both, ROW_AXES, axis=2, tiled=True)

    spread = jnp.pad(
        jnp.concatenate([routes, priority.reshape(-1, 1)], axis=1).reshape(
            group_rows // SEQ, SEQ, TOP + 1
        ),
        ((0, 0), (0, ROWS - SEQ), (0, 0)),
        constant_values=-1,
    ).reshape(tp_size, own_rows, TOP + 1)
    backward = (lax.axis_index("tp") - jnp.arange(tp_size) + tp_size) % tp_size
    spread = jnp.take(spread, backward, axis=0).reshape(total, TOP + 1)
    spread_t = spread.T
    slot_row, slot_col = call(
        partial(route_kernel, capacity),
        (shape((EXPERTS, total), jnp.int32), shape((total, LANES), jnp.int32)),
        "route",
    )(spread_t[TOP:], spread[:, TOP:], spread_t[:TOP], spread[:, :TOP])
    slot_row = slot_row.reshape(EXPERTS, 1, total)

    in_smem = pl.BlockSpec(memory_space=pltpu.SMEM)
    in_vmem = pl.BlockSpec(memory_space=pltpu.VMEM)
    a_two, y_one, proj, context, pack_all = call(
        partial(forward_kernel, places, block),
        (
            shape((own_rows, D), low_type),
            shape((own_rows, D), full_type),
            shape((own_rows, 3 * D), low_type),
            shape((own_rows, D), low_type),
            shape((D, WIDE), low_type),
        ),
        "attend_forward",
        in_specs=[in_smem] + [in_vmem] * (1 + len(pieces)),
    )(offsets, tok_pad, *pieces)

    row_parts = collect(a_two)

    slot_row_spec = pl.BlockSpec((1, 1, total), lambda e: (e, 0, 0))
    slot_col_spec = pl.BlockSpec((total, LANES), lambda e: (0, 0))
    part_spec = pl.BlockSpec((own_rows, D), lambda e: (0, 0))
    grad_spec = pl.BlockSpec((own_rows + 2 * EXPERTS, D), lambda e: (0, 0))
    in_spec = pl.BlockSpec((1, slots, D), lambda e: (e, 0, 0))
    mid_spec = pl.BlockSpec((1, slots, hidden_width), lambda e: (e, 0, 0))
    up_spec = pl.BlockSpec((1, 1, D, hidden_width), lambda e: (0, e, 0, 0))
    down_spec = pl.BlockSpec((1, 1, D, hidden_width), lambda e: (1, e, 0, 0))
    pack_spec = pl.BlockSpec((D, WIDE), lambda e: (0, 0))

    cot_slots = call(
        partial(gather_kernel, tp_size),
        shape((EXPERTS, slots, D), low_type),
        "gather_cotangent",
        grid=(EXPERTS,),
        in_specs=[slot_row_spec] + [part_spec] * tp_size,
        out_specs=in_spec,
        scratch_shapes=[pltpu.VMEM((total, D), low_type)],
    )(slot_row, *cot_parts)

    expert_in, weighted, grad_pre, *grad_parts = call(
        partial(experts_kernel, tp_size),
        [
            shape((EXPERTS, slots, D), low_type),
            shape((EXPERTS, slots, hidden_width), low_type),
            shape((EXPERTS, slots, hidden_width), low_type),
        ]
        + [shape((own_rows + 2 * EXPERTS, D), low_type)] * tp_size,
        "experts",
        grid=(EXPERTS,),
        in_specs=[slot_row_spec, slot_col_spec, in_spec, up_spec, down_spec, pack_spec]
        + [part_spec] * tp_size,
        out_specs=[in_spec, mid_spec, mid_spec] + [grad_spec] * tp_size,
        scratch_shapes=[
            pltpu.VMEM((total, D), low_type),
            pltpu.VMEM((EXPERTS, total), full_type),
            pltpu.VMEM((EXPERTS, total), full_type),
            pltpu.VMEM((total, D), full_type),
        ],
    )(slot_row, slot_col, cot_slots, both_all, both_all, pack_all, *row_parts)

    grad_arrived = deliver(grad_parts)

    grad_both = call(
        weights_kernel,
        shape((EXPERTS, 2, D, hidden_width), low_type),
        "expert_weights",
        grid=(EXPERTS,),
        in_specs=[in_spec, in_spec, mid_spec, mid_spec],
        out_specs=pl.BlockSpec((1, 2, D, hidden_width), lambda e: (e, 0, 0, 0)),
    )(expert_in, cot_slots, weighted, grad_pre)
    grad_both = lax.psum_scatter(grad_both, ROW_AXES, scatter_dimension=2, tiled=True)

    combined = call(
        combine_kernel,
        [shape((own_rows, D), low_type)] * tp_size,
        "combine",
        grid=(EXPERTS,),
        in_specs=[slot_col_spec, mid_spec, down_spec],
        out_specs=[part_spec] * tp_size,
        scratch_shapes=[pltpu.VMEM((total, D), full_type)],
    )(slot_col, weighted, both_all)

    *combined, grad_arrived[-1] = lax.optimization_barrier((*combined, grad_arrived[-1]))
    moe_arrived = deliver(combined)

    grad_tokens, *grad_packs = call(
        partial(backward_kernel, tp_size, block),
        [shape((own_rows, D), low_type)] + grad_shapes,
        "attend_backward",
        in_specs=[in_smem] + [in_vmem] * (7 + tp_size),
        scratch_shapes=[
            pltpu.VMEM((D, WIDE), low_type),
            pltpu.VMEM((own_rows, 3 * D), low_type),
            pltpu.VMEM((own_rows, D), low_type),
        ],
    )(offsets, a_two, y_one, cot_pad, context, proj, tok_pad, pack_all, *grad_arrived)

    reduced = reduce_near(*grad_packs) if near else reduce_far(*grad_packs)
    moe_rows = sum(part.astype(full_type) for part in moe_arrived)
    output = drop_padding((y_one + moe_rows).astype(low_type))
    grad_both = grad_both.astype(full_type)
    return (
        output,
        drop_padding(grad_tokens),
        reduced[:, : 3 * D],
        reduced[:, 3 * D : SIDE],
        reduced[:, SIDE : SIDE + EXPERTS],
        reduced[:, SIDE + 8],
        reduced[:, SIDE + 9],
        reduced[:, SIDE + 10],
        reduced[:, SIDE + 11],
        grad_both[:, 0],
        grad_both[:, 1],
    )


def solution(mesh):
    rows = P(ALL_AXES, None)
    vector = P(ALL_AXES)
    weights = P(None, ROW_AXES, "tp")
    group = P(ROW_AXES, None)
    in_specs = (rows,) * 4 + (vector,) * 4 + (weights,) * 2 + (group,) * 2 + (rows,)
    out_specs = (rows,) * 5 + (vector,) * 4 + (weights,) * 2
    return jax.shard_map(
        on_device, mesh=mesh, in_specs=in_specs, out_specs=out_specs, check_vma=False
    )
```

```python
from functools import partial
import math

import jax
import jax.numpy as jnp
from jax import lax
from jax.experimental import pallas as pl
from jax.experimental.pallas import tpu as pltpu
from jax.sharding import PartitionSpec as P


D = 512
HEADS = 8
HEAD = 64
SEQ = 197
TOP = 2
EXPERTS = 8

LANES = 128
ROWS = 208
WIDE = 3 * D + D + LANES
SIDE = 4 * D

epsilon = 1e-06
low_type = jnp.bfloat16
full_type = jnp.float32
ALL_AXES = ("fsdp", "ctx", "tp")
ROW_AXES = ("fsdp", "ctx")
VMEM_LIMIT = 58 * 1024 * 1024


def norm_forward(values):
    center = values - jnp.mean(values, axis=-1, keepdims=True)
    spread = jnp.mean(center * center, axis=-1, keepdims=True)
    inv_scale = lax.rsqrt(spread + epsilon)
    return (center * inv_scale, inv_scale)


def norm_backward(grad_norm, normed, inv_scale, gain_row):
    scaled = grad_norm * gain_row
    centred = scaled - jnp.mean(scaled, axis=-1, keepdims=True)
    return inv_scale * (centred - normed * jnp.mean(scaled * normed, axis=-1, keepdims=True))


def mul(left, right):
    return jnp.dot(left, right, preferred_element_type=full_type)


def rows_product(left, right):
    return lax.dot_general(
        left, right, (((0,), (0,)), ((), ())), preferred_element_type=full_type
    )


def times_transpose(left, right):
    return lax.dot_general(
        left, right, (((1,), (1,)), ((), ())), preferred_element_type=full_type
    )


def call(kernel, out_shape, **options):
    return pl.pallas_call(
        kernel,
        out_shape=out_shape,
        compiler_params=pltpu.CompilerParams(vmem_limit_bytes=VMEM_LIMIT),
        **options,
    )


def shape(dims, kind):
    return jax.ShapeDtypeStruct(dims, kind)


def route_kernel(
    capacity, order_row, order_col, routes_row, routes_col, slot_row_ref, slot_col_ref
):
    total = order_row.shape[1]
    first, second = routes_col[:, 0:1], routes_col[:, 1:2]
    lane = lax.broadcasted_iota(jnp.int32, (total, LANES), 1)
    picks_first = (first == lane).astype(full_type)
    picks_second = (second == lane).astype(full_type)
    picks = jnp.concatenate([picks_first, picks_second], axis=1).astype(low_type)
    count_first = jnp.sum(picks_first, axis=0, keepdims=True)
    row = lax.broadcasted_iota(jnp.int32, (EXPERTS, total), 0)
    first_row, second_row = routes_row[0:1, :], routes_row[1:2, :]
    across_first = (first_row == row).astype(full_type)
    across_second = (second_row == row).astype(full_type)
    across = jnp.concatenate([across_first, across_second], axis=0).astype(low_type)
    count_across = jnp.sum(across_first, axis=1, keepdims=True)
    bound = jnp.float32(capacity)
    for start in range(0, total, LANES):
        block = pl.ds(start, LANES)
        earlier = (order_row[...] < order_col[block, :]).astype(full_type).astype(low_type)
        counts = mul(earlier, picks)
        mine, other = routes_col[block, 0:1], routes_col[block, 1:2]
        lane_b = lax.broadcasted_iota(jnp.int32, (LANES, LANES), 1)
        slot = jnp.where(
            mine == lane_b,
            counts[:, :LANES],
            jnp.where(other == lane_b, counts[:, LANES:] + count_first, -1.0),
        )
        slot_col_ref[block, :] = jnp.where(slot < bound, slot, -1.0).astype(jnp.int32)
        counts_t = times_transpose(across, earlier)
        row_b = lax.broadcasted_iota(jnp.int32, (EXPERTS, LANES), 0)
        slot_t = jnp.where(
            routes_row[0:1, block] == row_b,
            counts_t[:EXPERTS, :],
            jnp.where(
                routes_row[1:2, block] == row_b, counts_t[EXPERTS:, :] + count_across, -1.0
            ),
        )
        slot_row_ref[:, block] = jnp.where(slot_t < bound, slot_t, -1.0).astype(jnp.int32)


def dispatch_mask(slot_row, slots):
    total = slot_row.shape[-1]
    return lax.broadcasted_iota(jnp.int32, (slots, total), 0) == slot_row


def combine_mask(slot_col, expert, slots):
    total = slot_col.shape[0]
    lane = lax.broadcasted_iota(jnp.int32, (total, LANES), 1)
    mine = jnp.sum(jnp.where(lane == expert, slot_col, 0), axis=1, keepdims=True)
    return lax.broadcasted_iota(jnp.int32, (total, slots), 1) == mine


def as_low(mask):
    return mask.astype(full_type).astype(low_type)


def join_parts(part_refs, whole):
    own = part_refs[0].shape[0]
    for index, part in enumerate(part_refs):
        whole[index * own : (index + 1) * own, :] = part[...]


def gather_kernel(parts, slot_row_ref, *refs):
    part_refs, (out_ref, whole) = refs[:parts], refs[parts:]

    @pl.when(pl.program_id(0) == 0)
    def _():
        join_parts(part_refs, whole)

    mask = dispatch_mask(slot_row_ref[0], out_ref.shape[1])
    out_ref[0] = mul(as_low(mask), whole[...]).astype(low_type)


def side_rows(pack_ref):
    return jnp.transpose(pack_ref[:, SIDE:].astype(full_type))


def experts_kernel(parts, slot_row_ref, slot_col_ref, cot_ref, up_ref, down_ref, side_ref, *refs):
    part_refs, refs = refs[:parts], refs[parts:]
    (rows_out, weighted_out, grad_pre_out), refs = refs[:3], refs[3:]
    group_outs, (rows_ref, gates, grad_gates, total_acc) = refs[:parts], refs[parts:]
    expert = pl.program_id(0)
    slots = cot_ref.shape[1]

    @pl.when(expert == 0)
    def _():
        join_parts(part_refs, rows_ref)
        route_t = side_rows(side_ref)[:EXPERTS].astype(low_type)
        logits = times_transpose(route_t, rows_ref[...])
        raised = jnp.exp(logits - jnp.max(logits, axis=0, keepdims=True))
        gates[...] = raised / jnp.sum(raised, axis=0, keepdims=True)
        total_acc[...] = jnp.zeros_like(total_acc)

    mask = dispatch_mask(slot_row_ref[0], slots)
    expert_in = mul(as_low(mask), rows_ref[...]).astype(low_type)
    gate_row = gates[pl.ds(expert, 1), :]
    weight = jnp.sum(jnp.where(mask, gate_row, 0.0), axis=1, keepdims=True)
    pre = mul(expert_in, up_ref[0, 0])
    grad_hidden = mul(cot_ref[0], down_ref[0, 0])
    slope = math.sqrt(2.0 / math.pi)
    square = pre * pre
    bent = jnp.tanh(slope * (pre + 0.044715 * (pre * square)))
    half = 0.5 * (1.0 + bent)
    hidden = (pre * half).astype(low_type).astype(full_type)
    pull = half + 0.5 * pre * (1.0 - bent * bent) * (slope * (1.0 + (3 * 0.044715) * square))
    grad_weight = jnp.sum(hidden * grad_hidden, axis=1, keepdims=True)
    grad_gates[pl.ds(expert, 1), :] = jnp.sum(
        jnp.where(mask, grad_weight, 0.0), axis=0, keepdims=True
    )
    grad_pre = (weight * grad_hidden * pull).astype(low_type)
    rows_out[0] = expert_in
    weighted_out[0] = (weight * hidden).astype(low_type)
    grad_pre_out[0] = grad_pre
    grad_in = times_transpose(grad_pre, up_ref[0, 0]).astype(low_type)
    back = as_low(combine_mask(slot_col_ref[...], expert, slots))
    total_acc[...] += mul(back, grad_in)

    @pl.when(expert == EXPERTS - 1)
    def _():
        own = part_refs[0].shape[0]
        total = rows_ref.shape[0]
        for index, out in enumerate(group_outs):
            out[:own, :] = total_acc[index * own : (index + 1) * own, :].astype(low_type)
            gates_part = pltpu.roll(grad_gates[...], (total - index * own) % total, 1)[:, :D]
            high = gates_part.astype(low_type).astype(full_type)
            pair = jnp.concatenate([high, gates_part - high], axis=0)
            out[own:, :] = pair.astype(low_type)


def weights_kernel(rows_ref, cot_ref, weighted_ref, grad_pre_ref, out_ref):
    out_ref[0, 0] = rows_product(rows_ref[0], grad_pre_ref[0]).astype(low_type)
    out_ref[0, 1] = rows_product(cot_ref[0], weighted_ref[0]).astype(low_type)


def combine_kernel(slot_col_ref, weighted_ref, down_ref, *refs):
    outs, total_acc = refs[:-1], refs[-1]
    expert = pl.program_id(0)

    @pl.when(expert == 0)
    def _():
        total_acc[...] = jnp.zeros_like(total_acc)

    expert_out = times_transpose(weighted_ref[0], down_ref[0, 0]).astype(low_type)
    back = as_low(combine_mask(slot_col_ref[...], expert, weighted_ref.shape[1]))
    total_acc[...] += mul(back, expert_out)

    @pl.when(expert == EXPERTS - 1)
    def _():
        own = outs[0].shape[0]
        for index, out in enumerate(outs):
            out[...] = total_acc[index * own : (index + 1) * own, :].astype(low_type)


def head_masks():
    lane = lax.broadcasted_iota(jnp.int32, (1, LANES), 1)
    left = (lane < HEAD).astype(full_type).astype(low_type)
    return (left, 1.0 - left)


def softmax_rows(queries, keys):
    scores = times_transpose(queries, keys) * (1.0 / math.sqrt(HEAD))
    column = lax.broadcasted_iota(jnp.int32, scores.shape, 1)
    scores = jnp.where(column < SEQ, scores, -1e30)
    raised = jnp.exp(scores - jnp.max(scores, axis=-1, keepdims=True))
    return raised / jnp.sum(raised, axis=-1, keepdims=True)


def head_pairs(images):
    for image in range(images):
        rows = pl.ds(image * ROWS, ROWS)
        for pair in range(HEADS * HEAD // LANES):
            yield rows, tuple(
                pl.ds(part * D + pair * LANES, LANES) for part in range(3)
            )


def forward_kernel(places, block, offset_ref, tokens_ref, *refs):
    pieces, (a_two_ref, y_ref, proj_ref, context_ref, pack_ref) = refs[:-5], refs[-5:]
    for piece, place in zip(pieces, places):
        for index, at in enumerate(place):
            start = pl.multiple_of(offset_ref[at], block)
            pack_ref[pl.ds(start, block), :] = piece[index * block : (index + 1) * block, :]
    side = side_rows(pack_ref)
    values = tokens_ref[...].astype(full_type)
    images = tokens_ref.shape[0] // ROWS
    normed, _ = norm_forward(values)
    a_one = (normed * side[8:9] + side[9:10]).astype(low_type)
    proj_ref[...] = mul(a_one, pack_ref[:, : 3 * D]).astype(low_type)
    masks = head_masks()
    lane = lax.broadcasted_iota(jnp.int32, (ROWS, LANES), 1)
    for rows, (q_at, k_at, v_at) in head_pairs(images):
        queries, keys, vals = proj_ref[rows, q_at], proj_ref[rows, k_at], proj_ref[rows, v_at]
        both = [
            mul(softmax_rows(queries * mask, keys).astype(low_type), vals) for mask in masks
        ]
        context_ref[rows, q_at] = jnp.where(lane < HEAD, both[0], both[1]).astype(low_type)
    y_one = values + mul(context_ref[...], pack_ref[:, 3 * D : SIDE])
    y_ref[...] = y_one
    normed_two, _ = norm_forward(y_one)
    a_two_ref[...] = (normed_two * side[10:11] + side[11:12]).astype(low_type)


def backward_kernel(
    parts,
    block,
    offset_ref,
    a_two_ref,
    y_ref,
    cot_ref,
    context_ref,
    proj_ref,
    tokens_ref,
    pack_ref,
    *refs,
):
    grad_refs, grad_tokens_ref, outs = refs[:parts], refs[parts], refs[parts + 1 : -3]
    grad_pack_ref, grad_proj, grad_context = refs[-3:]
    side = side_rows(pack_ref)
    gain_a, offset_a, gain_b = side[8:9], side[9:10], side[10:11]
    route_t = side[:EXPERTS].astype(low_type)
    a_two = a_two_ref[...]
    images = a_two.shape[0] // ROWS
    logits = times_transpose(route_t, a_two)
    raised = jnp.exp(logits - jnp.max(logits, axis=0, keepdims=True))
    gates = raised / jnp.sum(raised, axis=0, keepdims=True)
    own = a_two.shape[0]
    arrived = grad_refs[0][...].astype(full_type)
    for part in grad_refs[1:]:
        arrived += part[...].astype(full_type)
    grad_gates = arrived[own : own + EXPERTS, :own] + arrived[own + EXPERTS :, :own]
    grad_logits = (
        gates * (grad_gates - jnp.sum(gates * grad_gates, axis=0, keepdims=True))
    ).astype(low_type)
    grad_route = mul(grad_logits, a_two)
    grad_a_two = arrived[:own] + rows_product(grad_logits, route_t)
    normed_two, inv_two = norm_forward(y_ref[...])
    grad_gain_b = jnp.sum(grad_a_two * normed_two, axis=0, keepdims=True)
    grad_offset_b = jnp.sum(grad_a_two, axis=0, keepdims=True)
    grad_y = cot_ref[...].astype(full_type) + norm_backward(
        grad_a_two, normed_two, inv_two, gain_b
    )
    grad_branch = grad_y.astype(low_type)
    grad_pack_ref[:, 3 * D : SIDE] = rows_product(context_ref[...], grad_branch).astype(low_type)
    grad_context[...] = times_transpose(grad_branch, pack_ref[:, 3 * D : SIDE]).astype(low_type)
    masks = head_masks()
    scale = 1.0 / math.sqrt(HEAD)
    for rows, (q_at, k_at, v_at) in head_pairs(images):
        queries, keys, vals = proj_ref[rows, q_at], proj_ref[rows, k_at], proj_ref[rows, v_at]
        grads = grad_context[rows, q_at]
        grad_q, grad_k, grad_v = 0.0, 0.0, 0.0
        for mask in masks:
            own_q, own_k, own_g = queries * mask, keys * mask, grads * mask
            probs = softmax_rows(own_q, keys)
            grad_probs = times_transpose(own_g, vals)
            dots = jnp.sum(probs * grad_probs, axis=-1, keepdims=True)
            grad_scores = (probs * (grad_probs - dots)).astype(low_type)
            grad_v += rows_product(probs.astype(low_type), own_g)
            grad_q += mul(grad_scores, own_k)
            grad_k += rows_product(grad_scores, own_q)
        grad_proj[rows, q_at] = (grad_q * scale).astype(low_type)
        grad_proj[rows, k_at] = (grad_k * scale).astype(low_type)
        grad_proj[rows, v_at] = grad_v.astype(low_type)
    values = tokens_ref[...].astype(full_type)
    normed_one, inv_one = norm_forward(values)
    a_one = (normed_one * gain_a + offset_a).astype(low_type)
    grad_pack_ref[:, : 3 * D] = rows_product(a_one, grad_proj[...]).astype(low_type)
    grad_a_one = times_transpose(grad_proj[...], pack_ref[:, : 3 * D])
    grad_gain_a = jnp.sum(grad_a_one * normed_one, axis=0, keepdims=True)
    grad_offset_a = jnp.sum(grad_a_one, axis=0, keepdims=True)
    grad_tokens_ref[...] = (
        grad_y + norm_backward(grad_a_one, normed_one, inv_one, gain_a)
    ).astype(low_type)
    row = lax.broadcasted_iota(jnp.int32, (EXPERTS, D), 0)
    norms = jnp.where(
        row == 0,
        grad_gain_a,
        jnp.where(
            row == 1,
            grad_offset_a,
            jnp.where(row == 2, grad_gain_b, jnp.where(row == 3, grad_offset_b, 0.0)),
        ),
    )
    spare = jnp.zeros((LANES - 2 * EXPERTS, D), full_type)
    sides = jnp.concatenate([grad_route, norms, spare], axis=0)
    grad_pack_ref[:, SIDE:] = jnp.transpose(sides).astype(low_type)
    at = 0
    for out in outs:
        for index in range(out.shape[0] // block):
            start = pl.multiple_of(offset_ref[at], block)
            out[index * block : (index + 1) * block, :] = grad_pack_ref[pl.ds(start, block), :]
            at += 1


def pad_images(rows):
    width = rows.shape[-1]
    images = rows.shape[0] // SEQ
    apart = rows.reshape(images, SEQ, width)
    return jnp.pad(apart, ((0, 0), (0, ROWS - SEQ), (0, 0))).reshape(images * ROWS, width)


def drop_padding(rows):
    width = rows.shape[-1]
    images = rows.shape[0] // ROWS
    return rows.reshape(images, ROWS, width)[:, :SEQ].reshape(images * SEQ, width)


def swap(blocks, axis_name):
    return lax.all_to_all(blocks, axis_name, 0, 0, tiled=True)


def add_up(blocks, axis_name):
    return jnp.sum(swap(blocks, axis_name).astype(full_type), axis=0)


def rotate(value, axis_name, step):
    size = lax.axis_size(axis_name)
    return lax.ppermute(value, axis_name, [(i, (i + step) % size) for i in range(size)])


def cross(value, axis_name, bit):
    size = lax.axis_size(axis_name)
    return lax.ppermute(value, axis_name, [(i, i ^ bit) for i in range(size)])


def collect(part):
    others = range(1, lax.axis_size("tp"))
    return [part] + [rotate(part, "tp", step) for step in others]


def deliver(parts):
    return parts[:1] + [rotate(part, "tp", -step) for step, part in enumerate(parts) if step]


def near_mesh():
    return lax.axis_size("fsdp") == 2 and lax.axis_size("ctx") == 4 and lax.axis_size("tp") == 4


def pack_offsets(block):
    spot = jnp.arange(32, dtype=jnp.int32)
    core, y, x, back = spot // 16, spot // 8 % 2, spot // 4 % 2, spot % 4
    row = (lax.axis_index("fsdp") ^ y) * 4 + (lax.axis_index("ctx") ^ (2 * x + core))
    return ((row * 4 + (lax.axis_index("tp") - back + 4) % 4) * block).astype(jnp.int32)


def gather_near(pack):
    column = jnp.concatenate(collect(pack), axis=0)
    half = column.shape[0] // 2
    over_x = cross(column, "ctx", 2)
    over_y = cross(column, "fsdp", 1)
    low_half = cross(over_y[:half], "ctx", 2)
    high_half = cross(over_x[half:], "fsdp", 1)
    pieces = [column, over_x, over_y, low_half, high_half]
    pieces += [cross(piece, "ctx", 1) for piece in pieces]
    places = [range(0, 4), range(4, 8), range(8, 12), range(12, 14), range(14, 16)]
    places += [[spot + 16 for spot in place] for place in places]
    return pieces, [list(place) for place in places]


def add_low(left, right):
    return (left.astype(full_type) + right.astype(full_type)).astype(low_type)


def reduce_near(own, other):
    rest = (own.shape[0] // 16, own.shape[1])
    sums = add_low(own, cross(other, "ctx", 1)).reshape((2, 2, 4) + rest)
    far = sums[1, 1]
    by_x = cross(far[:2], "ctx", 2)
    by_y = cross(far[2:], "fsdp", 1)
    to_y = jnp.concatenate([add_low(sums[1, 0, :2], by_x), sums[1, 0, 2:]], axis=0)
    to_x = jnp.concatenate([sums[0, 1, :2], add_low(sums[0, 1, 2:], by_y)], axis=0)
    near_x = cross(to_x, "ctx", 2)
    near_y = cross(to_y, "fsdp", 1)
    column = add_low(add_low(sums[0, 0], near_x), near_y)
    arrived = deliver([column[step] for step in range(4)])
    return sum(part.astype(full_type) for part in arrived)


def gather_far(pack):
    wide = lax.all_gather(pack, "tp", axis=0, tiled=True)
    return [lax.all_gather(wide, ROW_AXES, axis=0, tiled=True)], [[0]]


def reduce_far(grad_pack):
    sizes = tuple(lax.axis_size(name) for name in ALL_AXES)
    own = grad_pack.shape[0] // math.prod(sizes)
    rest = (own, grad_pack.shape[1])
    blocks = grad_pack.reshape(sizes + rest)
    blocks = add_up(jnp.moveaxis(blocks, 1, 0), "ctx").astype(low_type)
    blocks = add_up(jnp.moveaxis(blocks, 1, 0), "tp").astype(low_type)
    return add_up(blocks, "fsdp")


def block_step(
    tokens,
    w_qkv,
    w_attend,
    w_route,
    gain_one,
    shift_one,
    gain_two,
    shift_two,
    w_up,
    w_down,
    routes,
    priority,
    cotangent,
):
    tok_rows = tokens.shape[0]
    tp_size = lax.axis_size("tp")
    images = tok_rows // SEQ
    own_rows = images * ROWS
    group_rows = tok_rows * tp_size
    total = own_rows * tp_size
    capacity = group_rows * TOP * 5 // (4 * EXPERTS)
    slots = -(-capacity // 16) * 16
    hidden_width = w_up.shape[2]

    columns = [w_qkv, w_attend, w_route]
    columns += [v[:, None] for v in (gain_one, shift_one, gain_two, shift_two)]
    pack = jnp.concatenate(columns, axis=1).astype(low_type)
    pack = jnp.pad(pack, ((0, 0), (0, WIDE - pack.shape[1])))
    near = near_mesh()
    if near:
        block = pack.shape[0]
        offsets = pack_offsets(block)
        pieces, places = gather_near(pack)
        half = D // 2
        grad_shapes = [shape((half, WIDE), low_type)] * 2
    else:
        block = D
        offsets = jnp.zeros((1,), jnp.int32)
        pieces, places = gather_far(pack)
        grad_shapes = [shape((D, WIDE), low_type)]

    cotangent, w_up, w_down, pieces[0] = lax.optimization_barrier(
        (cotangent, w_up, w_down, pieces[0])
    )
    cot_pad = pad_images(cotangent)
    tok_pad = pad_images(tokens)
    cot_parts = collect(cot_pad)
    both = jnp.stack([w_up, w_down]).astype(low_type)
    both_all = lax.all_gather(both, ROW_AXES, axis=2, tiled=True)

    spread = jnp.pad(
        jnp.concatenate([routes, priority.reshape(-1, 1)], axis=1).reshape(
            group_rows // SEQ, SEQ, TOP + 1
        ),
        ((0, 0), (0, ROWS - SEQ), (0, 0)),
        constant_values=-1,
    ).reshape(tp_size, own_rows, TOP + 1)
    twice = jnp.concatenate([spread[::-1], spread[::-1]], axis=0)
    spread = lax.dynamic_slice_in_dim(twice, tp_size - 1 - lax.axis_index("tp"), tp_size, 0)
    spread = spread.reshape(total, TOP + 1)
    spread_t = spread.T
    slot_row, slot_col = call(
        partial(route_kernel, capacity),
        (shape((EXPERTS, total), jnp.int32), shape((total, LANES), jnp.int32)),
    )(spread_t[TOP:], spread[:, TOP:], spread_t[:TOP], spread[:, :TOP])
    slot_row = slot_row.reshape(EXPERTS, 1, total)

    in_smem = pl.BlockSpec(memory_space=pltpu.SMEM)
    in_vmem = pl.BlockSpec(memory_space=pltpu.VMEM)
    a_two, y_one, proj, context, pack_all = call(
        partial(forward_kernel, places, block),
        (
            shape((own_rows, D), low_type),
            shape((own_rows, D), full_type),
            shape((own_rows, 3 * D), low_type),
            shape((own_rows, D), low_type),
            shape((D, WIDE), low_type),
        ),
        in_specs=[in_smem] + [in_vmem] * (1 + len(pieces)),
    )(offsets, tok_pad, *pieces)

    row_parts = collect(a_two)

    slot_row_spec = pl.BlockSpec((1, 1, total), lambda e: (e, 0, 0))
    slot_col_spec = pl.BlockSpec((total, LANES), lambda e: (0, 0))
    part_spec = pl.BlockSpec((own_rows, D), lambda e: (0, 0))
    grad_spec = pl.BlockSpec((own_rows + 2 * EXPERTS, D), lambda e: (0, 0))
    in_spec = pl.BlockSpec((1, slots, D), lambda e: (e, 0, 0))
    mid_spec = pl.BlockSpec((1, slots, hidden_width), lambda e: (e, 0, 0))
    up_spec = pl.BlockSpec((1, 1, D, hidden_width), lambda e: (0, e, 0, 0))
    down_spec = pl.BlockSpec((1, 1, D, hidden_width), lambda e: (1, e, 0, 0))
    pack_spec = pl.BlockSpec((D, WIDE), lambda e: (0, 0))

    cot_slots = call(
        partial(gather_kernel, tp_size),
        shape((EXPERTS, slots, D), low_type),
        grid=(EXPERTS,),
        in_specs=[slot_row_spec] + [part_spec] * tp_size,
        out_specs=in_spec,
        scratch_shapes=[pltpu.VMEM((total, D), low_type)],
    )(slot_row, *cot_parts)

    expert_in, weighted, grad_pre, *grad_parts = call(
        partial(experts_kernel, tp_size),
        [
            shape((EXPERTS, slots, D), low_type),
            shape((EXPERTS, slots, hidden_width), low_type),
            shape((EXPERTS, slots, hidden_width), low_type),
        ]
        + [shape((own_rows + 2 * EXPERTS, D), low_type)] * tp_size,
        grid=(EXPERTS,),
        in_specs=[slot_row_spec, slot_col_spec, in_spec, up_spec, down_spec, pack_spec]
        + [part_spec] * tp_size,
        out_specs=[in_spec, mid_spec, mid_spec] + [grad_spec] * tp_size,
        scratch_shapes=[
            pltpu.VMEM((total, D), low_type),
            pltpu.VMEM((EXPERTS, total), full_type),
            pltpu.VMEM((EXPERTS, total), full_type),
            pltpu.VMEM((total, D), full_type),
        ],
    )(slot_row, slot_col, cot_slots, both_all, both_all, pack_all, *row_parts)

    grad_arrived = deliver(grad_parts)

    grad_both = call(
        weights_kernel,
        shape((EXPERTS, 2, D, hidden_width), low_type),
        grid=(EXPERTS,),
        in_specs=[in_spec, in_spec, mid_spec, mid_spec],
        out_specs=pl.BlockSpec((1, 2, D, hidden_width), lambda e: (e, 0, 0, 0)),
    )(expert_in, cot_slots, weighted, grad_pre)
    grad_both = lax.psum_scatter(grad_both, ROW_AXES, scatter_dimension=2, tiled=True)

    combined = call(
        combine_kernel,
        [shape((own_rows, D), low_type)] * tp_size,
        grid=(EXPERTS,),
        in_specs=[slot_col_spec, mid_spec, down_spec],
        out_specs=[part_spec] * tp_size,
        scratch_shapes=[pltpu.VMEM((total, D), full_type)],
    )(slot_col, weighted, both_all)

    combined, grad_arrived = lax.optimization_barrier((list(combined), grad_arrived))
    moe_arrived = deliver(combined)

    grad_tokens, *grad_packs = call(
        partial(backward_kernel, tp_size, block),
        [shape((own_rows, D), low_type)] + grad_shapes,
        in_specs=[in_smem] + [in_vmem] * (7 + tp_size),
        scratch_shapes=[
            pltpu.VMEM((D, WIDE), low_type),
            pltpu.VMEM((own_rows, 3 * D), low_type),
            pltpu.VMEM((own_rows, D), low_type),
        ],
    )(offsets, a_two, y_one, cot_pad, context, proj, tok_pad, pack_all, *grad_arrived)

    reduced = reduce_near(*grad_packs) if near else reduce_far(*grad_packs)
    moe_rows = sum(part.astype(full_type) for part in moe_arrived)
    output = drop_padding((y_one + moe_rows).astype(low_type))
    grad_both = grad_both.astype(full_type)
    return (
        output,
        drop_padding(grad_tokens),
        reduced[:, : 3 * D],
        reduced[:, 3 * D : SIDE],
        reduced[:, SIDE : SIDE + EXPERTS],
        reduced[:, SIDE + 8],
        reduced[:, SIDE + 9],
        reduced[:, SIDE + 10],
        reduced[:, SIDE + 11],
        grad_both[:, 0],
        grad_both[:, 1],
    )


def solution(mesh):
    rows = P(ALL_AXES, None)
    vector = P(ALL_AXES)
    weights = P(None, ROW_AXES, "tp")
    group = P(ROW_AXES, None)
    in_specs = (rows,) * 4 + (vector,) * 4 + (weights,) * 2 + (group,) * 2 + (rows,)
    out_specs = (rows,) * 5 + (vector,) * 4 + (weights,) * 2
    return jax.shard_map(
        block_step, mesh=mesh, in_specs=in_specs, out_specs=out_specs, check_vma=False
    )
```

```python
from functools import partial
import math

import jax
import jax.numpy as jnp
from jax import lax
from jax.experimental import pallas as pl
from jax.experimental.pallas import tpu as pltpu
from jax.sharding import PartitionSpec as P


D = 512
HEADS = 8
HEAD = 64
SEQ = 197
TOP = 2
EXPERTS = 8

LANES = 128
ROWS = 208
WIDE = 3 * D + D + LANES
SIDE = 4 * D

epsilon = 1e-06
low_type = jnp.bfloat16
full_type = jnp.float32
ALL_AXES = ("fsdp", "ctx", "tp")
ROW_AXES = ("fsdp", "ctx")
VMEM_LIMIT = 58 * 1024 * 1024


def norm_forward(values):
    center = values - jnp.mean(values, axis=-1, keepdims=True)
    spread = jnp.mean(center * center, axis=-1, keepdims=True)
    inv_scale = lax.rsqrt(spread + epsilon)
    return (center * inv_scale, inv_scale)


def norm_backward(grad_norm, normed, inv_scale, gain_row):
    scaled = grad_norm * gain_row
    centred = scaled - jnp.mean(scaled, axis=-1, keepdims=True)
    return inv_scale * (centred - normed * jnp.mean(scaled * normed, axis=-1, keepdims=True))


def mul(left, right):
    return jnp.dot(left, right, preferred_element_type=full_type)


def rows_product(left, right):
    return lax.dot_general(
        left, right, (((0,), (0,)), ((), ())), preferred_element_type=full_type
    )


def times_transpose(left, right):
    return lax.dot_general(
        left, right, (((1,), (1,)), ((), ())), preferred_element_type=full_type
    )


def call(kernel, out_shape, **options):
    return pl.pallas_call(
        kernel,
        out_shape=out_shape,
        compiler_params=pltpu.CompilerParams(vmem_limit_bytes=VMEM_LIMIT),
        **options,
    )


def shape(dims, kind):
    return jax.ShapeDtypeStruct(dims, kind)


def route_kernel(
    capacity, order_row, order_col, routes_row, routes_col, slot_row_ref, slot_col_ref
):
    total = order_row.shape[1]
    first, second = routes_col[:, 0:1], routes_col[:, 1:2]
    lane = lax.broadcasted_iota(jnp.int32, (total, LANES), 1)
    picks_first = (first == lane).astype(full_type)
    picks_second = (second == lane).astype(full_type)
    picks = jnp.concatenate([picks_first, picks_second], axis=1).astype(low_type)
    count_first = jnp.sum(picks_first, axis=0, keepdims=True)
    row = lax.broadcasted_iota(jnp.int32, (EXPERTS, total), 0)
    first_row, second_row = routes_row[0:1, :], routes_row[1:2, :]
    across_first = (first_row == row).astype(full_type)
    across_second = (second_row == row).astype(full_type)
    across = jnp.concatenate([across_first, across_second], axis=0).astype(low_type)
    count_across = jnp.sum(across_first, axis=1, keepdims=True)
    bound = jnp.float32(capacity)
    for start in range(0, total, LANES):
        block = pl.ds(start, LANES)
        earlier = (order_row[...] < order_col[block, :]).astype(full_type).astype(low_type)
        counts = mul(earlier, picks)
        mine, other = routes_col[block, 0:1], routes_col[block, 1:2]
        lane_b = lax.broadcasted_iota(jnp.int32, (LANES, LANES), 1)
        slot = jnp.where(
            mine == lane_b,
            counts[:, :LANES],
            jnp.where(other == lane_b, counts[:, LANES:] + count_first, -1.0),
        )
        slot_col_ref[block, :] = jnp.where(slot < bound, slot, -1.0).astype(jnp.int32)
        counts_t = times_transpose(across, earlier)
        row_b = lax.broadcasted_iota(jnp.int32, (EXPERTS, LANES), 0)
        slot_t = jnp.where(
            routes_row[0:1, block] == row_b,
            counts_t[:EXPERTS, :],
            jnp.where(
                routes_row[1:2, block] == row_b, counts_t[EXPERTS:, :] + count_across, -1.0
            ),
        )
        slot_row_ref[:, block] = jnp.where(slot_t < bound, slot_t, -1.0).astype(jnp.int32)


def dispatch_mask(slot_row, slots):
    total = slot_row.shape[-1]
    return lax.broadcasted_iota(jnp.int32, (slots, total), 0) == slot_row


def combine_mask(slot_col, expert, slots):
    total = slot_col.shape[0]
    lane = lax.broadcasted_iota(jnp.int32, (total, LANES), 1)
    mine = jnp.sum(jnp.where(lane == expert, slot_col, 0), axis=1, keepdims=True)
    return lax.broadcasted_iota(jnp.int32, (total, slots), 1) == mine


def as_low(mask):
    return mask.astype(full_type).astype(low_type)


def join_parts(part_refs, whole):
    own = part_refs[0].shape[0]
    for index, part in enumerate(part_refs):
        whole[index * own : (index + 1) * own, :] = part[...]


def gather_kernel(parts, slot_row_ref, *refs):
    part_refs, (out_ref, whole) = refs[:parts], refs[parts:]

    @pl.when(pl.program_id(0) == 0)
    def _():
        join_parts(part_refs, whole)

    mask = dispatch_mask(slot_row_ref[0], out_ref.shape[1])
    out_ref[0] = mul(as_low(mask), whole[...]).astype(low_type)


def side_rows(pack_ref):
    return jnp.transpose(pack_ref[:, SIDE:].astype(full_type))


def gates_of(route_t, rows):
    logits = times_transpose(route_t, rows)
    raised = jnp.exp(logits - jnp.max(logits, axis=0, keepdims=True))
    return raised / jnp.sum(raised, axis=0, keepdims=True)


def early_kernel(parts, slot_row_ref, side_ref, *refs):
    part_refs, (out_ref, gates_ref, whole) = refs[:parts], refs[parts:]

    @pl.when(pl.program_id(0) == 0)
    def _():
        filled = parts * part_refs[0].shape[0]
        join_parts(part_refs, whole)
        whole[filled:, :] = jnp.zeros((whole.shape[0] - filled, D), low_type)
        gates_ref[...] = gates_of(side_rows(side_ref)[:EXPERTS].astype(low_type), whole[...])

    mask = dispatch_mask(slot_row_ref[0][:, : whole.shape[0]], out_ref.shape[1])
    out_ref[0] = mul(as_low(mask), whole[...]).astype(low_type)


def experts_kernel(
    slot_row_ref,
    cot_ref,
    up_ref,
    down_ref,
    side_ref,
    early_ref,
    early_gates,
    last_ref,
    rows_out,
    weighted_out,
    grad_pre_out,
    grad_in_out,
    grad_gates_out,
    rows_ref,
    gates,
):
    expert = pl.program_id(0)
    slots = cot_ref.shape[1]
    total = slot_row_ref.shape[2]
    tail = rows_ref.shape[0]
    base = total - tail

    @pl.when(expert == 0)
    def _():
        own = last_ref.shape[0]
        overlap = early_gates.shape[1] - base
        rows_ref[: tail - own, :] = jnp.zeros((tail - own, D), low_type)
        rows_ref[tail - own :, :] = last_ref[...]
        late = gates_of(side_rows(side_ref)[:EXPERTS].astype(low_type), rows_ref[...])
        gates[:, :base] = early_gates[:, :base]
        if overlap:
            lane = lax.broadcasted_iota(jnp.int32, (EXPERTS, overlap), 1)
            gates[:, base : base + overlap] = jnp.where(
                lane < tail - own, early_gates[:, base:], late[:, :overlap]
            )
        gates[:, base + overlap :] = late[:, overlap:]

    mask = dispatch_mask(slot_row_ref[0], slots)
    expert_in = early_ref[0] + mul(as_low(mask[:, base:]), rows_ref[...]).astype(low_type)
    gate_row = gates[pl.ds(expert, 1), :]
    weight = jnp.sum(jnp.where(mask, gate_row, 0.0), axis=1, keepdims=True)
    pre = mul(expert_in, up_ref[0, 0])
    grad_hidden = mul(cot_ref[0], down_ref[0, 0])
    slope = math.sqrt(2.0 / math.pi)
    square = pre * pre
    bent = jnp.tanh(slope * (pre + 0.044715 * (pre * square)))
    half = 0.5 * (1.0 + bent)
    hidden = (pre * half).astype(low_type).astype(full_type)
    pull = half + 0.5 * pre * (1.0 - bent * bent) * (slope * (1.0 + (3 * 0.044715) * square))
    grad_weight = jnp.sum(hidden * grad_hidden, axis=1, keepdims=True)
    grad_gates_out[pl.ds(expert, 1), :] = jnp.sum(
        jnp.where(mask, grad_weight, 0.0), axis=0, keepdims=True
    )
    grad_pre = (weight * grad_hidden * pull).astype(low_type)
    rows_out[0] = expert_in
    weighted_out[0] = (weight * hidden).astype(low_type)
    grad_pre_out[0] = grad_pre
    grad_in_out[0] = times_transpose(grad_pre, up_ref[0, 0]).astype(low_type)


def back_kernel(blocks, slot_col_ref, grad_in_ref, grad_gates_ref, *refs):
    outs, total_acc = refs[:-1], refs[-1]
    expert = pl.program_id(0)
    own = total_acc.shape[0] // len(blocks)
    total = slot_col_ref.shape[0]

    @pl.when(expert == 0)
    def _():
        total_acc[...] = jnp.zeros_like(total_acc)

    for index, at in enumerate(blocks):
        rows = slice(index * own, (index + 1) * own)
        slot_col = slot_col_ref[at * own : (at + 1) * own, :]
        back = as_low(combine_mask(slot_col, expert, grad_in_ref.shape[1]))
        total_acc[rows, :] += mul(back, grad_in_ref[0])

    @pl.when(expert == EXPERTS - 1)
    def _():
        for index, (at, out) in enumerate(zip(blocks, outs)):
            out[:own, :] = total_acc[index * own : (index + 1) * own, :].astype(low_type)
            shift = (total - at * own) % total
            gates_part = pltpu.roll(grad_gates_ref[...], shift, 1)[:, :D]
            high = gates_part.astype(low_type).astype(full_type)
            pair = jnp.concatenate([high, gates_part - high], axis=0)
            out[own:, :] = pair.astype(low_type)


def weights_kernel(rows_ref, cot_ref, weighted_ref, grad_pre_ref, out_ref):
    out_ref[0, 0] = rows_product(rows_ref[0], grad_pre_ref[0]).astype(low_type)
    out_ref[0, 1] = rows_product(cot_ref[0], weighted_ref[0]).astype(low_type)


def combine_kernel(slot_col_ref, weighted_ref, down_ref, *refs):
    outs, total_acc = refs[:-1], refs[-1]
    expert = pl.program_id(0)

    @pl.when(expert == 0)
    def _():
        total_acc[...] = jnp.zeros_like(total_acc)

    expert_out = times_transpose(weighted_ref[0], down_ref[0, 0]).astype(low_type)
    back = as_low(combine_mask(slot_col_ref[...], expert, weighted_ref.shape[1]))
    total_acc[...] += mul(back, expert_out)

    @pl.when(expert == EXPERTS - 1)
    def _():
        own = outs[0].shape[0]
        for index, out in enumerate(outs):
            out[...] = total_acc[index * own : (index + 1) * own, :].astype(low_type)


def head_masks():
    lane = lax.broadcasted_iota(jnp.int32, (1, LANES), 1)
    left = (lane < HEAD).astype(full_type).astype(low_type)
    return (left, 1.0 - left)


def softmax_rows(queries, keys):
    scores = times_transpose(queries, keys) * (1.0 / math.sqrt(HEAD))
    column = lax.broadcasted_iota(jnp.int32, scores.shape, 1)
    scores = jnp.where(column < SEQ, scores, -1e30)
    raised = jnp.exp(scores - jnp.max(scores, axis=-1, keepdims=True))
    return raised / jnp.sum(raised, axis=-1, keepdims=True)


def head_pairs(images):
    for image in range(images):
        rows = pl.ds(image * ROWS, ROWS)
        for pair in range(HEADS * HEAD // LANES):
            yield rows, tuple(
                pl.ds(part * D + pair * LANES, LANES) for part in range(3)
            )


def forward_kernel(places, block, offset_ref, tokens_ref, *refs):
    pieces, (a_two_ref, y_ref, proj_ref, context_ref, pack_ref) = refs[:-5], refs[-5:]
    for piece, place in zip(pieces, places):
        for index, at in enumerate(place):
            start = pl.multiple_of(offset_ref[at], block)
            pack_ref[pl.ds(start, block), :] = piece[index * block : (index + 1) * block, :]
    side = side_rows(pack_ref)
    values = tokens_ref[...].astype(full_type)
    images = tokens_ref.shape[0] // ROWS
    normed, _ = norm_forward(values)
    a_one = (normed * side[8:9] + side[9:10]).astype(low_type)
    proj_ref[...] = mul(a_one, pack_ref[:, : 3 * D]).astype(low_type)
    masks = head_masks()
    lane = lax.broadcasted_iota(jnp.int32, (ROWS, LANES), 1)
    for rows, (q_at, k_at, v_at) in head_pairs(images):
        queries, keys, vals = proj_ref[rows, q_at], proj_ref[rows, k_at], proj_ref[rows, v_at]
        both = [
            mul(softmax_rows(queries * mask, keys).astype(low_type), vals) for mask in masks
        ]
        context_ref[rows, q_at] = jnp.where(lane < HEAD, both[0], both[1]).astype(low_type)
    y_one = values + mul(context_ref[...], pack_ref[:, 3 * D : SIDE])
    y_ref[...] = y_one
    normed_two, _ = norm_forward(y_one)
    a_two_ref[...] = (normed_two * side[10:11] + side[11:12]).astype(low_type)


def backward_kernel(
    parts,
    block,
    offset_ref,
    a_two_ref,
    y_ref,
    cot_ref,
    context_ref,
    proj_ref,
    tokens_ref,
    pack_ref,
    *refs,
):
    grad_refs, grad_tokens_ref, outs = refs[:parts], refs[parts], refs[parts + 1 : -3]
    grad_pack_ref, grad_proj, grad_context = refs[-3:]
    side = side_rows(pack_ref)
    gain_a, offset_a, gain_b = side[8:9], side[9:10], side[10:11]
    route_t = side[:EXPERTS].astype(low_type)
    a_two = a_two_ref[...]
    images = a_two.shape[0] // ROWS
    logits = times_transpose(route_t, a_two)
    raised = jnp.exp(logits - jnp.max(logits, axis=0, keepdims=True))
    gates = raised / jnp.sum(raised, axis=0, keepdims=True)
    own = a_two.shape[0]
    arrived = grad_refs[0][...].astype(full_type)
    for part in grad_refs[1:]:
        arrived += part[...].astype(full_type)
    grad_gates = arrived[own : own + EXPERTS, :own] + arrived[own + EXPERTS :, :own]
    grad_logits = (
        gates * (grad_gates - jnp.sum(gates * grad_gates, axis=0, keepdims=True))
    ).astype(low_type)
    grad_route = mul(grad_logits, a_two)
    grad_a_two = arrived[:own] + rows_product(grad_logits, route_t)
    normed_two, inv_two = norm_forward(y_ref[...])
    grad_gain_b = jnp.sum(grad_a_two * normed_two, axis=0, keepdims=True)
    grad_offset_b = jnp.sum(grad_a_two, axis=0, keepdims=True)
    grad_y = cot_ref[...].astype(full_type) + norm_backward(
        grad_a_two, normed_two, inv_two, gain_b
    )
    grad_branch = grad_y.astype(low_type)
    grad_pack_ref[:, 3 * D : SIDE] = rows_product(context_ref[...], grad_branch).astype(low_type)
    grad_context[...] = times_transpose(grad_branch, pack_ref[:, 3 * D : SIDE]).astype(low_type)
    masks = head_masks()
    scale = 1.0 / math.sqrt(HEAD)
    for rows, (q_at, k_at, v_at) in head_pairs(images):
        queries, keys, vals = proj_ref[rows, q_at], proj_ref[rows, k_at], proj_ref[rows, v_at]
        grads = grad_context[rows, q_at]
        grad_q, grad_k, grad_v = 0.0, 0.0, 0.0
        for mask in masks:
            own_q, own_k, own_g = queries * mask, keys * mask, grads * mask
            probs = softmax_rows(own_q, keys)
            grad_probs = times_transpose(own_g, vals)
            dots = jnp.sum(probs * grad_probs, axis=-1, keepdims=True)
            grad_scores = (probs * (grad_probs - dots)).astype(low_type)
            grad_v += rows_product(probs.astype(low_type), own_g)
            grad_q += mul(grad_scores, own_k)
            grad_k += rows_product(grad_scores, own_q)
        grad_proj[rows, q_at] = (grad_q * scale).astype(low_type)
        grad_proj[rows, k_at] = (grad_k * scale).astype(low_type)
        grad_proj[rows, v_at] = grad_v.astype(low_type)
    values = tokens_ref[...].astype(full_type)
    normed_one, inv_one = norm_forward(values)
    a_one = (normed_one * gain_a + offset_a).astype(low_type)
    grad_pack_ref[:, : 3 * D] = rows_product(a_one, grad_proj[...]).astype(low_type)
    grad_a_one = times_transpose(grad_proj[...], pack_ref[:, : 3 * D])
    grad_gain_a = jnp.sum(grad_a_one * normed_one, axis=0, keepdims=True)
    grad_offset_a = jnp.sum(grad_a_one, axis=0, keepdims=True)
    grad_tokens_ref[...] = (
        grad_y + norm_backward(grad_a_one, normed_one, inv_one, gain_a)
    ).astype(low_type)
    row = lax.broadcasted_iota(jnp.int32, (EXPERTS, D), 0)
    norms = jnp.where(
        row == 0,
        grad_gain_a,
        jnp.where(
            row == 1,
            grad_offset_a,
            jnp.where(row == 2, grad_gain_b, jnp.where(row == 3, grad_offset_b, 0.0)),
        ),
    )
    spare = jnp.zeros((LANES - 2 * EXPERTS, D), full_type)
    sides = jnp.concatenate([grad_route, norms, spare], axis=0)
    grad_pack_ref[:, SIDE:] = jnp.transpose(sides).astype(low_type)
    at = 0
    for out in outs:
        for index in range(out.shape[0] // block):
            start = pl.multiple_of(offset_ref[at], block)
            out[index * block : (index + 1) * block, :] = grad_pack_ref[pl.ds(start, block), :]
            at += 1


def pad_images(rows):
    width = rows.shape[-1]
    images = rows.shape[0] // SEQ
    apart = rows.reshape(images, SEQ, width)
    return jnp.pad(apart, ((0, 0), (0, ROWS - SEQ), (0, 0))).reshape(images * ROWS, width)


def drop_padding(rows):
    width = rows.shape[-1]
    images = rows.shape[0] // ROWS
    return rows.reshape(images, ROWS, width)[:, :SEQ].reshape(images * SEQ, width)


def swap(blocks, axis_name):
    return lax.all_to_all(blocks, axis_name, 0, 0, tiled=True)


def add_up(blocks, axis_name):
    return jnp.sum(swap(blocks, axis_name).astype(full_type), axis=0)


def rotate(value, axis_name, step):
    size = lax.axis_size(axis_name)
    return lax.ppermute(value, axis_name, [(i, (i + step) % size) for i in range(size)])


def cross(value, axis_name, bit):
    size = lax.axis_size(axis_name)
    return lax.ppermute(value, axis_name, [(i, i ^ bit) for i in range(size)])


def steps():
    size = lax.axis_size("tp")
    nearest = [step for apart in range(1, size) for step in (apart, size - apart)]
    return list(dict.fromkeys([0] + nearest))


def collect(part):
    return [rotate(part, "tp", step) if step else part for step in steps()]


def deliver(parts):
    return [rotate(part, "tp", -step) if step else part for step, part in zip(steps(), parts)]


def near_mesh():
    return lax.axis_size("fsdp") == 2 and lax.axis_size("ctx") == 4 and lax.axis_size("tp") == 4


def pack_offsets(block):
    spot = jnp.arange(32, dtype=jnp.int32)
    core, y, x, back = spot // 16, spot // 8 % 2, spot // 4 % 2, spot % 4
    row = (lax.axis_index("fsdp") ^ y) * 4 + (lax.axis_index("ctx") ^ (2 * x + core))
    return ((row * 4 + (lax.axis_index("tp") - back + 4) % 4) * block).astype(jnp.int32)


def gather_near(pack):
    arrived = dict(zip(steps(), collect(pack)))
    column = jnp.concatenate([arrived[step] for step in range(4)], axis=0)
    half = column.shape[0] // 2
    over_x = cross(column, "ctx", 2)
    over_y = cross(column, "fsdp", 1)
    low_half = cross(over_y[:half], "ctx", 2)
    high_half = cross(over_x[half:], "fsdp", 1)
    pieces = [column, over_x, over_y, low_half, high_half]
    pieces += [cross(piece, "ctx", 1) for piece in pieces]
    places = [range(0, 4), range(4, 8), range(8, 12), range(12, 14), range(14, 16)]
    places += [[spot + 16 for spot in place] for place in places]
    return pieces, [list(place) for place in places]


def add_low(left, right):
    return (left.astype(full_type) + right.astype(full_type)).astype(low_type)


def reduce_near(own, other):
    rest = (own.shape[0] // 16, own.shape[1])
    sums = add_low(own, cross(other, "ctx", 1)).reshape((2, 2, 4) + rest)
    far = sums[1, 1]
    by_x = cross(far[:2], "ctx", 2)
    by_y = cross(far[2:], "fsdp", 1)
    to_y = jnp.concatenate([add_low(sums[1, 0, :2], by_x), sums[1, 0, 2:]], axis=0)
    to_x = jnp.concatenate([sums[0, 1, :2], add_low(sums[0, 1, 2:], by_y)], axis=0)
    near_x = cross(to_x, "ctx", 2)
    near_y = cross(to_y, "fsdp", 1)
    column = add_low(add_low(sums[0, 0], near_x), near_y)
    arrived = deliver([column[step] for step in steps()])
    return sum(part.astype(full_type) for part in arrived)


def gather_far(pack):
    wide = lax.all_gather(pack, "tp", axis=0, tiled=True)
    return [lax.all_gather(wide, ROW_AXES, axis=0, tiled=True)], [[0]]


def reduce_far(grad_pack):
    sizes = tuple(lax.axis_size(name) for name in ALL_AXES)
    own = grad_pack.shape[0] // math.prod(sizes)
    rest = (own, grad_pack.shape[1])
    blocks = grad_pack.reshape(sizes + rest)
    blocks = add_up(jnp.moveaxis(blocks, 1, 0), "ctx").astype(low_type)
    blocks = add_up(jnp.moveaxis(blocks, 1, 0), "tp").astype(low_type)
    return add_up(blocks, "fsdp")


def block_step(
    tokens,
    w_qkv,
    w_attend,
    w_route,
    gain_one,
    shift_one,
    gain_two,
    shift_two,
    w_up,
    w_down,
    routes,
    priority,
    cotangent,
):
    tok_rows = tokens.shape[0]
    tp_size = lax.axis_size("tp")
    images = tok_rows // SEQ
    own_rows = images * ROWS
    group_rows = tok_rows * tp_size
    total = own_rows * tp_size
    capacity = group_rows * TOP * 5 // (4 * EXPERTS)
    slots = -(-capacity // 16) * 16
    hidden_width = w_up.shape[2]

    columns = [w_qkv, w_attend, w_route]
    columns += [v[:, None] for v in (gain_one, shift_one, gain_two, shift_two)]
    pack = jnp.concatenate(columns, axis=1).astype(low_type)
    pack = jnp.pad(pack, ((0, 0), (0, WIDE - pack.shape[1])))
    near = near_mesh()
    if near:
        block = pack.shape[0]
        offsets = pack_offsets(block)
        pieces, places = gather_near(pack)
        half = D // 2
        grad_shapes = [shape((half, WIDE), low_type)] * 2
    else:
        block = D
        offsets = jnp.zeros((1,), jnp.int32)
        pieces, places = gather_far(pack)
        grad_shapes = [shape((D, WIDE), low_type)]

    cot_pad = pad_images(cotangent)
    tok_pad = pad_images(tokens)
    both = jnp.stack([w_up, w_down]).astype(low_type)
    cot_pad, both, pieces[0] = lax.optimization_barrier((cot_pad, both, pieces[0]))
    cot_parts = collect(cot_pad)
    both_all = lax.all_gather(both, ROW_AXES, axis=2, tiled=True)

    spread = jnp.pad(
        jnp.concatenate([routes, priority.reshape(-1, 1)], axis=1).reshape(
            group_rows // SEQ, SEQ, TOP + 1
        ),
        ((0, 0), (0, ROWS - SEQ), (0, 0)),
        constant_values=-1,
    ).reshape(tp_size, own_rows, TOP + 1)
    twice = jnp.concatenate([spread[::-1], spread[::-1]], axis=0)
    spread = lax.dynamic_slice_in_dim(twice, tp_size - 1 - lax.axis_index("tp"), tp_size, 0)
    spread = jnp.concatenate([spread[step] for step in steps()], axis=0)
    spread_t = spread.T
    slot_row, slot_col = call(
        partial(route_kernel, capacity),
        (shape((EXPERTS, total), jnp.int32), shape((total, LANES), jnp.int32)),
    )(spread_t[TOP:], spread[:, TOP:], spread_t[:TOP], spread[:, :TOP])
    slot_row = slot_row.reshape(EXPERTS, 1, total)

    in_smem = pl.BlockSpec(memory_space=pltpu.SMEM)
    in_vmem = pl.BlockSpec(memory_space=pltpu.VMEM)
    a_two, y_one, proj, context, pack_all = call(
        partial(forward_kernel, places, block),
        (
            shape((own_rows, D), low_type),
            shape((own_rows, D), full_type),
            shape((own_rows, 3 * D), low_type),
            shape((own_rows, D), low_type),
            shape((D, WIDE), low_type),
        ),
        in_specs=[in_smem] + [in_vmem] * (1 + len(pieces)),
    )(offsets, tok_pad, *pieces)

    row_parts = collect(a_two)

    slot_row_spec = pl.BlockSpec((1, 1, total), lambda e: (e, 0, 0))
    slot_col_spec = pl.BlockSpec((total, LANES), lambda e: (0, 0))
    part_spec = pl.BlockSpec((own_rows, D), lambda e: (0, 0))
    grad_spec = pl.BlockSpec((own_rows + 2 * EXPERTS, D), lambda e: (0, 0))
    in_spec = pl.BlockSpec((1, slots, D), lambda e: (e, 0, 0))
    mid_spec = pl.BlockSpec((1, slots, hidden_width), lambda e: (e, 0, 0))
    up_spec = pl.BlockSpec((1, 1, D, hidden_width), lambda e: (0, e, 0, 0))
    down_spec = pl.BlockSpec((1, 1, D, hidden_width), lambda e: (1, e, 0, 0))
    pack_spec = pl.BlockSpec((D, WIDE), lambda e: (0, 0))

    cot_slots = call(
        partial(gather_kernel, tp_size),
        shape((EXPERTS, slots, D), low_type),
        grid=(EXPERTS,),
        in_specs=[slot_row_spec] + [part_spec] * tp_size,
        out_specs=in_spec,
        scratch_shapes=[pltpu.VMEM((total, D), low_type)],
    )(slot_row, *cot_parts)

    early = tp_size - 1
    early_lanes = -(-early * own_rows // LANES) * LANES
    late_lanes = total - early * own_rows // LANES * LANES
    early_gates_spec = pl.BlockSpec((EXPERTS, early_lanes), lambda e: (0, 0))
    gates_spec = pl.BlockSpec((EXPERTS, total), lambda e: (0, 0))
    early_in, early_gates = call(
        partial(early_kernel, early),
        [
            shape((EXPERTS, slots, D), low_type),
            shape((EXPERTS, early_lanes), full_type),
        ],
        grid=(EXPERTS,),
        in_specs=[slot_row_spec, pack_spec] + [part_spec] * early,
        out_specs=[in_spec, early_gates_spec],
        scratch_shapes=[pltpu.VMEM((early_lanes, D), low_type)],
    )(slot_row, pack_all, *row_parts[:early])

    expert_in, weighted, grad_pre, grad_in, grad_gates = call(
        experts_kernel,
        [
            shape((EXPERTS, slots, D), low_type),
            shape((EXPERTS, slots, hidden_width), low_type),
            shape((EXPERTS, slots, hidden_width), low_type),
            shape((EXPERTS, slots, D), low_type),
            shape((EXPERTS, total), full_type),
        ],
        grid=(EXPERTS,),
        in_specs=[
            slot_row_spec,
            in_spec,
            up_spec,
            down_spec,
            pack_spec,
            in_spec,
            early_gates_spec,
            part_spec,
        ],
        out_specs=[in_spec, mid_spec, mid_spec, in_spec, gates_spec],
        scratch_shapes=[
            pltpu.VMEM((late_lanes, D), low_type),
            pltpu.VMEM((EXPERTS, total), full_type),
        ],
    )(slot_row, cot_slots, both_all, both_all, pack_all, early_in, early_gates, row_parts[-1])

    def back(blocks):
        return call(
            partial(back_kernel, blocks),
            [shape((own_rows + 2 * EXPERTS, D), low_type)] * len(blocks),
            grid=(EXPERTS,),
            in_specs=[slot_col_spec, in_spec, gates_spec],
            out_specs=[grad_spec] * len(blocks),
            scratch_shapes=[pltpu.VMEM((len(blocks) * own_rows, D), full_type)],
        )(slot_col, grad_in, grad_gates)

    grad_parts = back((0,)) + back(tuple(range(1, early)))
    grad_parts += back((early,))
    grad_arrived = deliver(grad_parts)

    grad_both = call(
        weights_kernel,
        shape((EXPERTS, 2, D, hidden_width), low_type),
        grid=(EXPERTS,),
        in_specs=[in_spec, in_spec, mid_spec, mid_spec],
        out_specs=pl.BlockSpec((1, 2, D, hidden_width), lambda e: (e, 0, 0, 0)),
    )(expert_in, cot_slots, weighted, grad_pre)
    grad_both = lax.psum_scatter(grad_both, ROW_AXES, scatter_dimension=2, tiled=True)

    combined = call(
        combine_kernel,
        [shape((own_rows, D), low_type)] * tp_size,
        grid=(EXPERTS,),
        in_specs=[slot_col_spec, mid_spec, down_spec],
        out_specs=[part_spec] * tp_size,
        scratch_shapes=[pltpu.VMEM((total, D), full_type)],
    )(slot_col, weighted, both_all)

    combined, grad_arrived = lax.optimization_barrier((list(combined), grad_arrived))
    moe_arrived = deliver(combined)

    grad_tokens, *grad_packs = call(
        partial(backward_kernel, tp_size, block),
        [shape((own_rows, D), low_type)] + grad_shapes,
        in_specs=[in_smem] + [in_vmem] * (7 + tp_size),
        scratch_shapes=[
            pltpu.VMEM((D, WIDE), low_type),
            pltpu.VMEM((own_rows, 3 * D), low_type),
            pltpu.VMEM((own_rows, D), low_type),
        ],
    )(offsets, a_two, y_one, cot_pad, context, proj, tok_pad, pack_all, *grad_arrived)

    reduced = reduce_near(*grad_packs) if near else reduce_far(*grad_packs)
    moe_rows = sum(part.astype(full_type) for part in moe_arrived)
    output = drop_padding((y_one + moe_rows).astype(low_type))
    grad_both = grad_both.astype(full_type)
    return (
        output,
        drop_padding(grad_tokens),
        reduced[:, : 3 * D],
        reduced[:, 3 * D : SIDE],
        reduced[:, SIDE : SIDE + EXPERTS],
        reduced[:, SIDE + 8],
        reduced[:, SIDE + 9],
        reduced[:, SIDE + 10],
        reduced[:, SIDE + 11],
        grad_both[:, 0],
        grad_both[:, 1],
    )


def solution(mesh):
    rows = P(ALL_AXES, None)
    vector = P(ALL_AXES)
    weights = P(None, ROW_AXES, "tp")
    group = P(ROW_AXES, None)
    in_specs = (rows,) * 4 + (vector,) * 4 + (weights,) * 2 + (group,) * 2 + (rows,)
    out_specs = (rows,) * 5 + (vector,) * 4 + (weights,) * 2
    return jax.shard_map(
        block_step, mesh=mesh, in_specs=in_specs, out_specs=out_specs, check_vma=False
    )
```
